256 devices in a mesh: gx: 16 (over x_hi, z), gy: 8 (over y, core), gz: 2 (over x_lo).
Axes of the slice: x: 4 (x_hi: 2, x_lo: 2; x = x_hi * 2 + x_lo), y: 4, z: 8, core: 2. Of those that a mesh axis runs over, the one named last changes fastest.
Arguments:
- populations: float32 [19, 64, 64, 256], P(None, 'gx', 'gy', 'gz'), may hold values from 0.015 to 0.49, as said below
- grain_velocity: float32 [3, 8192, 128], P(None, ('gx', 'gy', 'gz')), may hold values from -1.2 to 1.2
- grain_volume: float32 [8192, 128], P(('gx', 'gy', 'gz')), may hold values from 0.05 to 0.4
- slots: int32 [8192, 128], P(('gx', 'gy', 'gz')), may hold values 0 or 1
- contacts: int32 [8192, 32], P(('gx', 'gy', 'gz')), may hold values 0 or 1
- bin_cell: int32 [8192], P(('gx', 'gy', 'gz')), may hold values from 0 to 8191, as said below
Outputs:
- fluid: float32 [19, 64, 64, 256], P(None, 'gx', 'gy', 'gz')
- grains: float32 [3, 8192, 128], P(None, ('gx', 'gy', 'gz'))
The draws below stay inside these ranges and needn't reach their ends.
Inputs may be any that keep to these rules, and one draw needn't show every extreme that they name: `populations`: each part of the grid of one device holds distributions near w_i times a factor of order one. bin_cell[b] is a column index as in the reference program. A bin's column lies in the cells of the same index of gz as the device that holds the bin. Of the 32 bins that one device holds, at most 2 have columns in the cells of any one device, and in every draw every holder reaches 2 for some device.
All inputs are finite; a program needn't handle non-finite values. No bound on the sum of `slots` or of `contacts` on one device may be relied on, other than what follows from the above.
Results may differ from the reference program's by a relative error of at most 0.0001.
Values sent between devices are 32-bit elements; how exact they have to be, the bound alone decides.
A program may use at most 64 MiB of HBM per device.

```python
import math
import jax
import jax.numpy as jnp
import numpy as np
from jax import lax

CX = 4
CY = 8
CZ = 128
GRAINS = 128
BIN_DEV = 32
SUBSTEPS = 4
NX = 64
NY = 64
NZ = 256
NBINS = 8192


LATTICE_WEIGHTS = np.array([1.0 / 3.0] + [1.0 / 18.0] * 6 + [1.0 / 36.0] * 12)


def draw_populations(key, part):
    weights = jnp.asarray(LATTICE_WEIGHTS, jnp.float32).reshape(19, 1, 1, 1)
    factor = jax.random.uniform(key, (19, NX, NY, NZ), jnp.float32, 0.6, 1.4)
    return weights * factor


def draw_bin_cell(key, part):
    n_gx = NX // CX
    n_gy = NY // CY
    n_gz = NZ // CZ
    sources = n_gx * n_gy
    owners = sources * n_gz
    zblocks = CZ // GRAINS
    capacity = max(2, 4 * BIN_DEV // sources)
    keys = jax.random.split(key, 5)
    perms = jax.vmap(partial_perm(sources))(jax.random.split(keys[0], owners))
    orders = jax.vmap(partial_perm(BIN_DEV))(jax.random.split(keys[1], owners))
    place = jnp.arange(BIN_DEV, dtype=jnp.int32)
    group = jnp.where(place < capacity, 0, 1 + (place - capacity) % (sources - 1))
    group = group[orders]
    source = jnp.take_along_axis(perms, group, axis=1)
    owner_gz = (jnp.arange(owners, dtype=jnp.int32) % n_gz)[:, None]
    xcell = source // n_gy * CX + jax.random.randint(keys[2], (owners, BIN_DEV), 0, CX)
    ycell = source % n_gy * CY + jax.random.randint(keys[3], (owners, BIN_DEV), 0, CY)
    zblock = owner_gz * zblocks + jax.random.randint(keys[4], (owners, BIN_DEV), 0, zblocks)
    column = (xcell * NY + ycell) * (NZ // GRAINS) + zblock
    return column.reshape(-1).astype(jnp.int32)


def partial_perm(count):

    def permute(subkey):
        return jax.random.permutation(subkey, count).astype(jnp.int32)
    return permute


def touch_ends(values, rng, least, high):
    spot = [jax.random.randint(jax.random.fold_in(rng, axis), (), 0, length) for axis, length in enumerate(values.shape)]
    main_axis = values.shape.index(max(values.shape))
    next_to = spot[:main_axis] + [(spot[main_axis] + 1) % values.shape[main_axis]] + spot[main_axis + 1:]
    return values.at[tuple(spot)].set(least).at[tuple(next_to)].set(high)


def steps_of(stream_key, extent, pieces, low, largest):
    factor_of = 1.0
    for dim, shards_of in pieces:
        steps = jax.random.uniform(jax.random.fold_in(jax.random.fold_in(stream_key, 6), dim), (shards_of,), jnp.float32, low / len(pieces), largest / len(pieces))
        factor_of = factor_of * jnp.repeat(jnp.exp(steps), extent[dim] // shards_of).reshape((-1,) + (1,) * (len(extent) - 1 - dim))
    return factor_of


def noise(own_key, shape, scale, reach, shards=(), kind=jnp.bfloat16):
    values = scale * jax.random.normal(own_key, shape, jnp.float32)
    if shards:
        values = values * steps_of(own_key, shape, shards, -0.22, 0.18)
    return jnp.clip(values, -reach, reach).astype(kind)


def setup_inputs(seed: int = 0) -> dict:
    key_of = jax.random.split(jax.random.key(seed), 7)
    return {
        "populations": draw_populations(jax.random.fold_in(key_of[6], 71), 0),
        "grain_velocity": noise(key_of[1], (3, NBINS, GRAINS), 0.2, 1.2, ((1, 256),), jnp.float32),
        "grain_volume": jnp.clip(jnp.exp(math.log(0.4) - 2.0794415 * jax.random.uniform(key_of[2], (NBINS, GRAINS), jnp.float32) ** steps_of(key_of[2], (NBINS, GRAINS), ((0, 256),), -0.2, 0.2)), 0.05, 0.4),
        "slots": touch_ends((jax.random.randint(key_of[3], (NBINS, GRAINS), 0, 4) < 3).astype(jnp.int32), jax.random.fold_in(key_of[3], 1), 0, 1),
        "contacts": touch_ends((jax.random.randint(key_of[4], (NBINS, BIN_DEV), 0, 16) < 1).astype(jnp.int32), jax.random.fold_in(key_of[4], 1), 0, 1),
        "bin_cell": draw_bin_cell(jax.random.fold_in(key_of[6], 71), 0),
    }


VELOCITIES = np.array([[0, 0, 0], [1, 0, 0], [-1, 0, 0], [0, 1, 0], [0, -1, 0], [0, 0, 1], [0, 0, -1],
                       [1, 1, 0], [-1, -1, 0], [1, -1, 0], [-1, 1, 0],
                       [1, 0, 1], [-1, 0, -1], [1, 0, -1], [-1, 0, 1],
                       [0, 1, 1], [0, -1, -1], [0, 1, -1], [0, -1, 1]])
WEIGHTS = np.array([1.0 / 3.0] + [1.0 / 18.0] * 6 + [1.0 / 36.0] * 12)
OPPOSITE = [0, 2, 1, 4, 3, 6, 5, 8, 7, 10, 9, 12, 11, 14, 13, 16, 15, 18, 17]
relax_time = 0.8
contact_stiffness = 0.1
drag_factor = 2.0
gravity = 0.01


def moments(popul):
    density = jnp.sum(popul, axis=0)
    speed = []
    for axis in range(3):
        rising = np.array([i for i in range(19) if VELOCITIES[i, axis] == 1])
        falling = np.array([i for i in range(19) if VELOCITIES[i, axis] == -1])
        momentum = jnp.sum(popul[rising], axis=0) - jnp.sum(popul[falling], axis=0)
        speed.append(momentum / density)
    return density, speed


def grain_step(block, velocity, live, volume, links):
    grains = velocity.shape[2]
    bins = links.shape[1]
    groups = velocity.shape[1] // bins
    rate = drag_factor * volume * live
    drag = rate[None] * (block[:3] - velocity)
    moving = (velocity * live[None]).reshape(3, groups, bins, grains)
    pairs = links.reshape(groups, bins, bins)
    near = jnp.einsum('gkj,cgjs->cgks', pairs, moving, precision=lax.Precision.HIGHEST).reshape(3, -1, grains)
    count = jnp.einsum('gkj,gjs->gks', pairs, live.reshape(groups, bins, grains), precision=lax.Precision.HIGHEST).reshape(-1, grains)
    push = contact_stiffness * live[None] * (near - count[None] * velocity)
    fall = jnp.asarray([0.0, 0.0, gravity], jnp.float32).reshape(3, 1, 1) * live[None]
    updated = velocity + drag + push - fall
    forces = jnp.concatenate([-drag, (volume * live)[None]], axis=0)
    return updated, forces


def collide(popul, density, speed, field):
    scale = 1.0 / (1.0 + field[3])
    target = [scale * (speed[a] + relax_time * field[a] / density) for a in range(3)]
    square = target[0] * target[0] + target[1] * target[1] + target[2] * target[2]
    rows = []
    for i in range(19):
        along = jnp.zeros_like(density)
        for a in range(3):
            if VELOCITIES[i, a] != 0:
                along = along + float(VELOCITIES[i, a]) * target[a]
        equil = float(WEIGHTS[i]) * density * (1.0 + 3.0 * along + 4.5 * along * along - 1.5 * square)
        rows.append(popul[i] - (popul[i] - equil) / relax_time)
    return jnp.stack(rows)


def stream(post):
    depth = post.shape[3]
    zpos = jnp.arange(depth)
    rows = []
    for i in range(19):
        cx, cy, cz = int(VELOCITIES[i, 0]), int(VELOCITIES[i, 1]), int(VELOCITIES[i, 2])
        moved = jnp.roll(post[i], (cx, cy, cz), axis=(0, 1, 2))
        if cz == 1:
            moved = jnp.where(zpos == 0, post[OPPOSITE[i]], moved)
        elif cz == -1:
            moved = jnp.where(zpos == depth - 1, post[OPPOSITE[i]], moved)
        rows.append(moved)
    return jnp.stack(rows)


def reference(populations, grain_velocity, grain_volume, slots, contacts, bin_cell):
    live = slots.astype(jnp.float32)
    links = contacts.astype(jnp.float32)
    fluid = populations
    velocity = grain_velocity
    for step in range(SUBSTEPS):
        density, speed = moments(fluid)
        flow = jnp.stack(speed + [density]).reshape(4, -1, GRAINS)
        block = jnp.take(flow, bin_cell, axis=1)
        velocity, forces = grain_step(block, velocity, live, grain_volume, links)
        field = jnp.zeros_like(flow).at[:, bin_cell].add(forces).reshape(4, NX, NY, NZ)
        post = collide(fluid, density, speed, field)
        fluid = stream(post)
    return fluid, velocity
```

```python
import jax
import jax.numpy as jnp
import numpy as np
from jax import lax
from jax.experimental import pallas as pl
from jax.experimental.pallas import tpu as pltpu
from jax.sharding import PartitionSpec as P

SUBSTEPS = 4
VELOCITIES = [
    (0, 0, 0),
    (1, 0, 0), (-1, 0, 0), (0, 1, 0), (0, -1, 0), (0, 0, 1), (0, 0, -1),
    (1, 1, 0), (-1, -1, 0), (1, -1, 0), (-1, 1, 0),
    (1, 0, 1), (-1, 0, -1), (1, 0, -1), (-1, 0, 1),
    (0, 1, 1), (0, -1, -1), (0, 1, -1), (0, -1, 1),
]
WEIGHTS = [1.0 / 3.0] + [1.0 / 18.0] * 6 + [1.0 / 36.0] * 12
OPPOSITE = [0, 2, 1, 4, 3, 6, 5, 8, 7, 10, 9, 12, 11, 14, 13, 16, 15, 18, 17]
relax_time = 0.8
contact_stiffness = 0.1
drag_factor = 2.0
gravity = 0.01

X_UP = [1, 7, 9, 11, 13]
X_DOWN = [2, 8, 10, 12, 14]
Y_UP = [3, 7, 10, 15, 17]
Y_DOWN = [4, 8, 9, 16, 18]
Z_UP = [5, 11, 14, 15, 18]
Z_DOWN = [6, 13, 12, 17, 16]

F32 = jnp.float32
BF16 = jnp.bfloat16
MESH = pl.DeviceIdType.MESH


def split(x):
    high = x.astype(BF16)
    low = (x - high.astype(F32)).astype(BF16)
    return high, low


def kernel(
    n_gx, n_gy,
    pop, vel, vol, slots, contacts, cells,
    fluid, grains,
    post, fnow, pick_h, pick_ht, pick_c, pick_ct,
    id_out, id_in, u_out, u_in, w_out, w_in, halo_out, halo_in,
    id_ss, id_rs, u_ss, u_rs, w_ss, w_rs, h_ss, h_rs,
):
    devices = n_gx * n_gy
    n_xh, n_z, n_y, n_c = 2, n_gx // 2, n_gy // 2, 2
    gx, gy, gz = lax.axis_index("gx"), lax.axis_index("gy"), lax.axis_index("gz")
    me = gx * n_gy + gy
    xh, zc, yc, cc = gx // n_z, gx % n_z, gy // n_c, gy % n_c
    far = n_z // 2
    z_order = []
    for s in range(far, -1, -1):
        for d in (s, (n_z - s) % n_z):
            if d not in z_order:
                z_order.append(d)

    def to_all(act):
        groups = n_xh * n_y * n_c

        def dest(m, dz):
            px = (xh + m // (n_y * n_c)) % n_xh
            py = (yc + (m // n_c) % n_y) % n_y
            pc = (cc + m % n_c) % n_c
            pz = (zc + dz) % n_z
            return px * n_z + pz, py * n_c + pc

        def group(i, carry):
            for dz in z_order:
                act(*dest(groups - 1 - i, dz))
            return carry

        lax.fori_loop(0, groups - 1, group, 0)
        for dz in z_order:
            if dz != 0:
                act(*dest(0, dz))

    west, east = (gx + n_gx - 1) % n_gx, (gx + 1) % n_gx
    south, north = (gy + n_gy - 1) % n_gy, (gy + 1) % n_gy
    beyond = 1 - gz
    across = [(gx, gy), (east, gy), (west, gy), (gx, north), (gx, south)]

    barrier = pltpu.get_barrier_semaphore()

    def greet(px, py):
        pl.semaphore_signal(barrier, inc=1, device_id=(px, py, gz), device_id_type=MESH)

    to_all(greet)
    for px, py in across:
        pl.semaphore_signal(barrier, inc=1, device_id=(px, py, beyond), device_id_type=MESH)

    def exchange(out, inn, row, rows, ss, rs):
        here = pl.ds(row, rows)

        def copy(px, py):
            pltpu.make_async_remote_copy(
                src_ref=out.at[px * n_gy + py, here],
                dst_ref=inn.at[me, here],
                send_sem=ss,
                recv_sem=rs,
                device_id=(px, py, gz),
                device_id_type=MESH,
            ).start()

        to_all(copy)
        inn[me] = out[me]

    def whole(out, inn, row, rows, ss, rs):
        span = (pl.ds(0, devices - 1), pl.ds(row, rows))
        return pltpu.make_async_remote_copy(
            src_ref=out.at[span],
            dst_ref=inn.at[span],
            send_sem=ss,
            recv_sem=rs,
            device_id=(gx, gy, beyond),
            device_id_type=MESH,
        )

    sub = lax.broadcasted_iota(jnp.int32, (8, 128), 0)
    lane = lax.broadcasted_iota(jnp.int32, (8, 128), 1)
    matched = ((sub < 6) & (lane // 32 == sub % 3)) | ((sub >= 6) & (lane >= 96))
    slot_of = jnp.where(sub < 6, sub // 3, sub - 6)
    index = lane % 32

    cell = jnp.zeros((8, 128), jnp.int32)
    for b in range(32):
        cell = jnp.where(index == b, cells[b], cell)
    width = 8 * n_gy

    def source_of(c):
        column = c // 2
        return (column // width) // 4 * n_gy + (column % width) // 8

    source = source_of(cell)
    local = (cell // 2 // width) % 4 * 8 + (cell // 2 % width) % 8
    rank = jnp.zeros((8, 128), jnp.int32)
    for b in range(31):
        rank = rank + jnp.where((source == source_of(cells[b])) & (index > b), 1, 0)
    code = jnp.where(matched, 2 * source + rank - slot_of, -1000000)
    target = lax.broadcasted_iota(jnp.int32, (devices, 8, 128), 0) * 2
    hot = jnp.where(code[None] == target, 1.0, 0.0).astype(F32).reshape(devices * 8, 128)
    pick_h[:, 0:128] = hot.astype(BF16)
    pick_h[:, 128:256] = hot.astype(BF16)
    pick_ht[...] = hot.T.astype(BF16)

    def spread(pick, table):
        high, low = split(table)
        both = jnp.concatenate([high, low], axis=0)
        rows = jnp.dot(pick[...], both, preferred_element_type=F32)
        return rows.reshape(devices, 8, 128)

    def collect(pick_t, tiles, masked):
        rows = tiles.reshape(devices * 8, 128)
        if masked:
            inside = lax.broadcasted_iota(jnp.int32, (devices * 8, 128), 0) % 8 < 6
            rows = jnp.where(inside, rows, 0.0)
        high, low = split(rows)
        table = pick_t[...]
        return jnp.dot(table, high, preferred_element_type=F32) + jnp.dot(
            table, low, preferred_element_type=F32
        )

    column = lax.broadcasted_iota(jnp.int32, (128, 128), 0)
    lanes = lax.broadcasted_iota(jnp.int32, (128, 128), 1)
    own = jnp.where(column % 32 == lanes, jnp.broadcast_to(local[0:1] + 1, (128, 128)), 0)
    ids = jnp.sum(own.astype(F32), axis=1, keepdims=True)
    ids = jnp.where(column >= 96, jnp.broadcast_to(ids, (128, 128)), 0.0)
    id_out[...] = spread(pick_h, ids)

    live = slots[...].astype(F32)
    rate = drag_factor * vol[...] * live
    links = contacts[...].astype(F32).astype(BF16)
    count = jnp.dot(links, live.astype(BF16), preferred_element_type=F32)

    def weighted(v):
        return jnp.concatenate([rate * v[0], rate * v[1], rate * v[2], rate], axis=0)

    def near(moving):
        high, low = split(moving)
        return jnp.dot(links, high, preferred_element_type=F32) + jnp.dot(
            links, low, preferred_element_type=F32
        )

    velocity = [vel[a] for a in range(3)]
    w_out[0] = spread(pick_h, weighted(velocity))

    def moments(read):
        rho = jnp.zeros((32, 128), F32)
        momentum = [jnp.zeros((32, 128), F32) for _ in range(3)]
        for i in range(19):
            f = read(i)
            rho = rho + f
            for a in range(3):
                if VELOCITIES[i][a] == 1:
                    momentum[a] = momentum[a] + f
                elif VELOCITIES[i][a] == -1:
                    momentum[a] = momentum[a] - f
        return rho, [m / rho for m in momentum]

    def flow_rows(u):
        return jnp.concatenate([u[0], u[1], u[2], jnp.zeros((32, 128), F32)], axis=0)

    read_first = lambda i: pop[i].reshape(32, 128)
    read_next = lambda i: fnow[pl.ds(i * 32, 32), :]
    flow = moments(read_first)

    pl.semaphore_wait(barrier, devices - 1 + len(across))
    exchange(id_out, id_in, 6, 2, id_ss, id_rs)
    exchange(w_out.at[0], w_in.at[0], 0, 8, w_ss.at[0], w_rs.at[0])

    id_wait = whole(id_out, id_in, 6, 2, id_ss, id_rs)
    id_wait.wait_recv()
    first = jnp.broadcast_to(id_in[:, 6:7, :], (devices, 8, 128))
    second = jnp.broadcast_to(id_in[:, 7:8, :], (devices, 8, 128))
    held = jnp.where((slot_of == 0)[None], first, second)
    wanted = jnp.where(matched, index + 1, -1).astype(F32)
    hot_c = jnp.where(held == wanted[None], 1.0, 0.0).astype(F32).reshape(devices * 8, 128)
    pick_c[:, 0:128] = hot_c.astype(BF16)
    pick_c[:, 128:256] = hot_c.astype(BF16)

    def send_flow(t, u):
        u_out[t] = spread(pick_c, flow_rows(u))
        exchange(u_out.at[t], u_in.at[t], 0, 6, u_ss.at[t], u_rs.at[t])

    def wait_flow(t):
        whole(u_out.at[t], u_in.at[t], 0, 6, u_ss.at[t], u_rs.at[t]).wait_recv()

    def w_rows(t):
        return 8 if t == 0 else 6

    def send_weight(t, v):
        w_out[t] = spread(pick_h, weighted(v))
        exchange(w_out.at[t], w_in.at[t], 0, w_rows(t), w_ss.at[t], w_rs.at[t])

    def wait_weight(t):
        whole(w_out.at[t], w_in.at[t], 0, w_rows(t), w_ss.at[t], w_rs.at[t]).wait_recv()

    def advance(t, v):
        wait_flow(t)
        block = collect(pick_ht, u_in[t], True)
        updated = []
        for a in range(3):
            u = block[a * 32 : a * 32 + 32]
            drag = rate * (u - v[a])
            push = contact_stiffness * live * (near(v[a] * live) - count * v[a])
            value = v[a] + drag + push
            if a == 2:
                value = value - gravity * live
            updated.append(value)
        return updated

    def halo_copy(t, first_out, tiles, first_in, px, py, pz):
        return pltpu.make_async_remote_copy(
            src_ref=halo_out.at[t, pl.ds(first_out, tiles)],
            dst_ref=halo_in.at[t, pl.ds(first_in, tiles)],
            send_sem=h_ss.at[t],
            recv_sem=h_rs.at[t],
            device_id=(px, py, pz),
            device_id_type=MESH,
        )

    def collide(t, read, flow, field):
        rho, speed = flow
        scale = 1.0 / (1.0 + 0.5 * field[3])
        force = [field[a] - field[3] * speed[a] for a in range(3)]
        target = [scale * (speed[a] + relax_time * force[a] / rho) for a in range(3)]
        square = target[0] * target[0] + target[1] * target[1] + target[2] * target[2]
        base = 1.0 - 1.5 * square
        for i in range(19):
            along = None
            for a in range(3):
                c = VELOCITIES[i][a]
                if c == 1:
                    along = target[a] if along is None else along + target[a]
                elif c == -1:
                    along = -target[a] if along is None else along - target[a]
            shape = base if along is None else base + along * (3.0 + 4.5 * along)
            f = read(i)
            post[pl.ds(i * 32, 32), :] = f - (f - WEIGHTS[i] * rho * shape) / relax_time

    def tile(i, x):
        return post[pl.ds(i * 32 + x * 8, 8), :]

    def send_halo(t):
        for n in range(5):
            halo_out[t, n] = tile(X_UP[n], 3)
            halo_out[t, 5 + n] = tile(X_DOWN[n], 0)
            half = pl.ds((n % 2) * 4, 4)
            halo_out[t, 10 + n // 2, half, :] = post[pl.ds(Y_UP[n] * 32 + 7, 4, stride=8), :]
            halo_out[t, 13 + n // 2, half, :] = post[pl.ds(Y_DOWN[n] * 32, 4, stride=8), :]
        halo_out[t, 12, 4:8, :] = jnp.zeros((4, 128), F32)
        halo_out[t, 15, 4:8, :] = jnp.zeros((4, 128), F32)
        packed = jnp.zeros((8, 128), F32)
        for n in range(5):
            for x in range(4):
                k = n * 4 + x
                up = pltpu.roll(tile(Z_UP[n], x), (k + 1) % 128, 1)
                down = pltpu.roll(tile(Z_DOWN[n], x), k, 1) if k else tile(Z_DOWN[n], x)
                packed = jnp.where(lane == k, jnp.where(gz == 0, up, down), packed)
        halo_out[t, 16] = packed
        halo_copy(t, 0, 5, 0, east, gy, gz).start()
        halo_copy(t, 5, 5, 5, west, gy, gz).start()
        halo_copy(t, 10, 3, 10, gx, north, gz).start()
        halo_copy(t, 13, 3, 13, gx, south, gz).start()
        halo_copy(t, 1, 1, 16, east, north, gz).start()
        halo_copy(t, 6, 1, 17, west, south, gz).start()
        halo_copy(t, 2, 1, 18, east, south, gz).start()
        halo_copy(t, 7, 1, 19, west, north, gz).start()
        for n, (px, py) in enumerate(across):
            halo_copy(t, 16, 1, 20 + n, px, py, beyond).start()

    def halo_whole(t):
        return pltpu.make_async_remote_copy(
            src_ref=halo_in.at[t],
            dst_ref=halo_in.at[t],
            send_sem=h_ss.at[t],
            recv_sem=h_rs.at[t],
            device_id=(gx, gy, beyond),
            device_id_type=MESH,
        )

    def stream(t, write):
        halo_whole(t).wait_recv()
        level = halo_in[t, 20]
        block_of = lane // 4
        from_west = pltpu.roll(halo_in[t, 21], 125, 1)
        from_east = pltpu.roll(halo_in[t, 22], 3, 1)
        right = jnp.where(lane % 4 == 0, from_west, pltpu.roll(level, 1, 1))
        left = jnp.where(lane % 4 == 3, from_east, pltpu.roll(level, 127, 1))
        upper = jnp.where(sub == 0, pltpu.roll(halo_in[t, 23], 1, 0), pltpu.roll(level, 1, 0))
        lower = jnp.where(sub == 7, pltpu.roll(halo_in[t, 24], 7, 0), pltpu.roll(level, 7, 0))
        ghost = jnp.where(block_of == 1, right, level)
        ghost = jnp.where(block_of == 2, left, ghost)
        ghost = jnp.where(block_of == 3, upper, ghost)
        ghost = jnp.where(block_of == 4, lower, ghost)

        for i in range(19):
            cx, cy, cz = VELOCITIES[i]
            for x in range(4):
                sx = x - cx
                inside = 0 <= sx < 4
                if inside:
                    value = tile(i, sx)
                elif cx == 1:
                    value = halo_in[t, X_UP.index(i)]
                else:
                    value = halo_in[t, 5 + X_DOWN.index(i)]
                if cy == 1:
                    n = Y_UP.index(i)
                    if inside:
                        row = jnp.broadcast_to(
                            halo_in[t, 10 + n // 2, pl.ds((n % 2) * 4 + sx, 1), :], (8, 128)
                        )
                    else:
                        row = jnp.broadcast_to(
                            halo_in[t, 16 if cx == 1 else 19, pl.ds(7, 1), :], (8, 128)
                        )
                    value = jnp.where(sub == 0, row, pltpu.roll(value, 1, 0))
                elif cy == -1:
                    n = Y_DOWN.index(i)
                    if inside:
                        row = jnp.broadcast_to(
                            halo_in[t, 13 + n // 2, pl.ds((n % 2) * 4 + sx, 1), :], (8, 128)
                        )
                    else:
                        row = jnp.broadcast_to(
                            halo_in[t, 18 if cx == 1 else 17, pl.ds(0, 1), :], (8, 128)
                        )
                    value = jnp.where(sub == 7, row, pltpu.roll(value, 7, 0))
                if cz != 0:
                    n = (Z_UP if cz == 1 else Z_DOWN).index(i)
                    k = n * 4 + x
                    edge = jnp.broadcast_to(ghost[:, k : k + 1], (8, 128))
                    wall = tile(OPPOSITE[i], x)
                    if cz == 1:
                        edge = jnp.where(gz == 1, edge, wall)
                        value = jnp.where(lane == 0, edge, pltpu.roll(value, 1, 1))
                    else:
                        edge = jnp.where(gz == 0, edge, wall)
                        value = jnp.where(lane == 127, edge, pltpu.roll(value, 127, 1))
                write(i, x, value)

    def write_next(i, x, value):
        fnow[pl.ds(i * 32 + x * 8, 8), :] = value

    def write_last(i, x, value):
        fluid[i, x] = value

    solid = None

    def fluid_step(t, read, flow, write):
        nonlocal solid
        wait_weight(t)
        table = collect(pick_ct, w_in[t], t > 0)
        if t == 0:
            solid = table[96:128]
        field = [table[a * 32 : a * 32 + 32] for a in range(3)] + [solid]
        collide(t, read, flow, field)
        send_halo(t)
        stream(t, write)

    send_flow(0, flow[1])
    pick_ct[...] = hot_c.T.astype(BF16)
    fluid_step(0, read_first, flow, write_next)
    flow = moments(read_next)
    send_flow(1, flow[1])
    velocity = advance(0, velocity)
    send_weight(1, velocity)
    velocity = advance(1, velocity)
    send_weight(2, velocity)
    fluid_step(1, read_next, flow, write_next)
    flow = moments(read_next)
    send_flow(2, flow[1])
    fluid_step(2, read_next, flow, write_next)
    flow = moments(read_next)
    send_flow(3, flow[1])
    velocity = advance(2, velocity)
    send_weight(3, velocity)
    velocity = advance(3, velocity)
    for a in range(3):
        grains[a] = velocity[a]
    fluid_step(3, read_next, flow, write_last)

    id_wait.wait_send()
    for t in range(SUBSTEPS):
        whole(u_out.at[t], u_in.at[t], 0, 6, u_ss.at[t], u_rs.at[t]).wait_send()
        whole(w_out.at[t], w_in.at[t], 0, w_rows(t), w_ss.at[t], w_rs.at[t]).wait_send()
        halo_whole(t).wait_send()


def solution(mesh):
    n_gx, n_gy = mesh.shape["gx"], mesh.shape["gy"]
    devices = n_gx * n_gy
    vmem = pl.BlockSpec(memory_space=pltpu.VMEM)
    smem = pl.BlockSpec(memory_space=pltpu.SMEM)
    dma = pltpu.SemaphoreType.DMA

    def body(populations, grain_velocity, grain_volume, slots, contacts, bin_cell):
        return pl.pallas_call(
            lambda *refs: kernel(n_gx, n_gy, *refs),
            out_shape=(
                jax.ShapeDtypeStruct(populations.shape, F32),
                jax.ShapeDtypeStruct(grain_velocity.shape, F32),
            ),
            in_specs=[vmem] * 5 + [smem],
            out_specs=(vmem, vmem),
            scratch_shapes=[
                pltpu.VMEM((608, 128), F32),
                pltpu.VMEM((608, 128), F32),
                pltpu.VMEM((devices * 8, 256), BF16),
                pltpu.VMEM((128, devices * 8), BF16),
                pltpu.VMEM((devices * 8, 256), BF16),
                pltpu.VMEM((128, devices * 8), BF16),
                pltpu.VMEM((devices, 8, 128), F32),
                pltpu.VMEM((devices, 8, 128), F32),
                pltpu.VMEM((SUBSTEPS, devices, 8, 128), F32),
                pltpu.VMEM((SUBSTEPS, devices, 8, 128), F32),
                pltpu.VMEM((SUBSTEPS, devices, 8, 128), F32),
                pltpu.VMEM((SUBSTEPS, devices, 8, 128), F32),
                pltpu.VMEM((SUBSTEPS, 17, 8, 128), F32),
                pltpu.VMEM((SUBSTEPS, 25, 8, 128), F32),
                dma,
                dma,
                dma((SUBSTEPS,)),
                dma((SUBSTEPS,)),
                dma((SUBSTEPS,)),
                dma((SUBSTEPS,)),
                dma((SUBSTEPS,)),
                dma((SUBSTEPS,)),
            ],
            compiler_params=pltpu.CompilerParams(
                collective_id=0, has_side_effects=True, vmem_limit_bytes=48 << 20
            ),
            name="bed",
        )(populations, grain_velocity, grain_volume, slots, contacts, bin_cell)

    every = ("gx", "gy", "gz")
    in_specs = (
        P(None, "gx", "gy", "gz"),
        P(None, every, None),
        P(every, None),
        P(every, None),
        P(every, None),
        P(every),
    )
    out_specs = (P(None, "gx", "gy", "gz"), P(None, every, None))
    return jax.shard_map(body, mesh=mesh, in_specs=in_specs, out_specs=out_specs, check_vma=False)
```

```python
import jax
import jax.numpy as jnp
import numpy as np
from jax import lax
from jax.experimental import pallas as pl
from jax.experimental.pallas import tpu as pltpu
from jax.sharding import PartitionSpec as P

SUBSTEPS = 4
VELOCITIES = [
    (0, 0, 0),
    (1, 0, 0), (-1, 0, 0), (0, 1, 0), (0, -1, 0), (0, 0, 1), (0, 0, -1),
    (1, 1, 0), (-1, -1, 0), (1, -1, 0), (-1, 1, 0),
    (1, 0, 1), (-1, 0, -1), (1, 0, -1), (-1, 0, 1),
    (0, 1, 1), (0, -1, -1), (0, 1, -1), (0, -1, 1),
]
WEIGHTS = [1.0 / 3.0] + [1.0 / 18.0] * 6 + [1.0 / 36.0] * 12
OPPOSITE = [0, 2, 1, 4, 3, 6, 5, 8, 7, 10, 9, 12, 11, 14, 13, 16, 15, 18, 17]
relax_time = 0.8
contact_stiffness = 0.1
drag_factor = 2.0
gravity = 0.01

X_UP = [1, 7, 9, 11, 13]
X_DOWN = [2, 8, 10, 12, 14]
Y_UP = [3, 7, 10, 15, 17]
Y_DOWN = [4, 8, 9, 16, 18]
Z_UP = [5, 11, 14, 15, 18]
Z_DOWN = [6, 13, 12, 17, 16]

F32 = jnp.float32
BF16 = jnp.bfloat16
MESH = pl.DeviceIdType.MESH


def split(x):
    high = x.astype(BF16)
    low = (x - high.astype(F32)).astype(BF16)
    return high, low


def kernel(
    n_gx, n_gy,
    pop, vel, vol, slots, contacts, cells,
    fluid, grains,
    post, fnow, pick_h, pick_ht, pick_c, pick_ct,
    id_out, id_in, u_out, u_in, w_out, w_in, halo_out, halo_in,
    id_ss, id_rs, u_ss, u_rs, w_ss, w_rs, h_ss, h_rs,
):
    devices = n_gx * n_gy
    n_xh, n_z, n_y, n_c = 2, n_gx // 2, n_gy // 2, 2
    gx, gy, gz = lax.axis_index("gx"), lax.axis_index("gy"), lax.axis_index("gz")
    me = gx * n_gy + gy
    xh, zc, yc, cc = gx // n_z, gx % n_z, gy // n_c, gy % n_c
    far = n_z // 2
    z_order = []
    for s in range(far, -1, -1):
        for d in (s, (n_z - s) % n_z):
            if d not in z_order:
                z_order.append(d)

    def to_all(act):
        groups = n_xh * n_y * n_c

        def dest(m, dz):
            px = (xh + m // (n_y * n_c)) % n_xh
            py = (yc + (m // n_c) % n_y) % n_y
            pc = (cc + m % n_c) % n_c
            pz = (zc + dz) % n_z
            return px * n_z + pz, py * n_c + pc

        def group(i, carry):
            for dz in z_order:
                act(*dest(groups - 1 - i, dz))
            return carry

        lax.fori_loop(0, groups - 1, group, 0)
        for dz in z_order:
            if dz != 0:
                act(*dest(0, dz))

    west, east = (gx + n_gx - 1) % n_gx, (gx + 1) % n_gx
    south, north = (gy + n_gy - 1) % n_gy, (gy + 1) % n_gy
    beyond = 1 - gz
    across = [(gx, gy), (east, gy), (west, gy), (gx, north), (gx, south)]

    barrier = pltpu.get_barrier_semaphore()

    def greet(px, py):
        pl.semaphore_signal(barrier, inc=1, device_id=(px, py, gz), device_id_type=MESH)

    to_all(greet)
    for px, py in across:
        pl.semaphore_signal(barrier, inc=1, device_id=(px, py, beyond), device_id_type=MESH)

    def exchange(out, inn, row, rows, ss, rs):
        here = pl.ds(row, rows)

        def copy(px, py):
            pltpu.make_async_remote_copy(
                src_ref=out.at[px * n_gy + py, here],
                dst_ref=inn.at[me, here],
                send_sem=ss,
                recv_sem=rs,
                device_id=(px, py, gz),
                device_id_type=MESH,
            ).start()

        to_all(copy)
        inn[me] = out[me]

    def whole(out, inn, row, rows, ss, rs):
        span = (pl.ds(0, devices - 1), pl.ds(row, rows))
        return pltpu.make_async_remote_copy(
            src_ref=out.at[span],
            dst_ref=inn.at[span],
            send_sem=ss,
            recv_sem=rs,
            device_id=(gx, gy, beyond),
            device_id_type=MESH,
        )

    sub = lax.broadcasted_iota(jnp.int32, (8, 128), 0)
    lane = lax.broadcasted_iota(jnp.int32, (8, 128), 1)
    matched = ((sub < 6) & (lane // 32 == sub % 3)) | ((sub >= 6) & (lane >= 96))
    slot_of = jnp.where(sub < 6, sub // 3, sub - 6)
    index = lane % 32

    cell = jnp.zeros((8, 128), jnp.int32)
    for b in range(32):
        cell = jnp.where(index == b, cells[b], cell)
    width = 8 * n_gy

    def source_of(c):
        column = c // 2
        return (column // width) // 4 * n_gy + (column % width) // 8

    source = source_of(cell)
    local = (cell // 2 // width) % 4 * 8 + (cell // 2 % width) % 8
    rank = jnp.zeros((8, 128), jnp.int32)
    for b in range(31):
        rank = rank + jnp.where((source == source_of(cells[b])) & (index > b), 1, 0)
    code = jnp.where(matched, 2 * source + rank - slot_of, -1000000)
    target = lax.broadcasted_iota(jnp.int32, (devices, 8, 128), 0) * 2
    hot = jnp.where(code[None] == target, 1.0, 0.0).astype(F32).reshape(devices * 8, 128)
    pick_h[:, 0:128] = hot.astype(BF16)
    pick_h[:, 128:256] = hot.astype(BF16)
    pick_ht[...] = hot.T.astype(BF16)

    def spread(pick, table):
        high, low = split(table)
        both = jnp.concatenate([high, low], axis=0)
        rows = jnp.dot(pick[...], both, preferred_element_type=F32)
        return rows.reshape(devices, 8, 128)

    def collect(pick_t, tiles, masked):
        rows = tiles.reshape(devices * 8, 128)
        if masked:
            inside = lax.broadcasted_iota(jnp.int32, (devices * 8, 128), 0) % 8 < 6
            rows = jnp.where(inside, rows, 0.0)
        high, low = split(rows)
        table = pick_t[...]
        return jnp.dot(table, high, preferred_element_type=F32) + jnp.dot(
            table, low, preferred_element_type=F32
        )

    column = lax.broadcasted_iota(jnp.int32, (128, 128), 0)
    lanes = lax.broadcasted_iota(jnp.int32, (128, 128), 1)
    own = jnp.where(column % 32 == lanes, jnp.broadcast_to(local[0:1] + 1, (128, 128)), 0)
    ids = jnp.sum(own.astype(F32), axis=1, keepdims=True)
    ids = jnp.where(column >= 96, jnp.broadcast_to(ids, (128, 128)), 0.0)
    id_out[...] = spread(pick_h, ids)

    live = slots[...].astype(F32)
    rate = drag_factor * vol[...] * live
    links = contacts[...].astype(F32).astype(BF16)
    count = jnp.dot(links, live.astype(BF16), preferred_element_type=F32)

    def weighted(v):
        return jnp.concatenate([rate * v[0], rate * v[1], rate * v[2], rate], axis=0)

    def contact_push(v):
        pushed = []
        for a in range(3):
            push = contact_stiffness * live * (near(v[a] * live) - count * v[a])
            pushed.append(push - gravity * live if a == 2 else push)
        return pushed

    def without_flow(v, pushed):
        return [(1.0 - rate) * v[a] + pushed[a] for a in range(3)]

    def near(moving):
        high, low = split(moving)
        return jnp.dot(links, high, preferred_element_type=F32) + jnp.dot(
            links, low, preferred_element_type=F32
        )

    velocity = [vel[a] for a in range(3)]
    w_out[0] = spread(pick_h, weighted(velocity))

    def moments(read):
        rho = jnp.zeros((32, 128), F32)
        momentum = [jnp.zeros((32, 128), F32) for _ in range(3)]
        for i in range(19):
            f = read(i)
            rho = rho + f
            for a in range(3):
                if VELOCITIES[i][a] == 1:
                    momentum[a] = momentum[a] + f
                elif VELOCITIES[i][a] == -1:
                    momentum[a] = momentum[a] - f
        return rho, [m / rho for m in momentum]

    def flow_rows(u):
        return jnp.concatenate([u[0], u[1], u[2], jnp.zeros((32, 128), F32)], axis=0)

    read_first = lambda i: pop[i].reshape(32, 128)
    read_next = lambda i: fnow[pl.ds(i * 32, 32), :]
    flow = moments(read_first)

    pl.semaphore_wait(barrier, devices - 1 + len(across))
    exchange(id_out, id_in, 6, 2, id_ss, id_rs)
    def w_rows(t):
        return 8 if t == 0 else 6

    exchange(w_out.at[0], w_in.at[0], 0, w_rows(0), w_ss.at[0], w_rs.at[0])

    id_wait = whole(id_out, id_in, 6, 2, id_ss, id_rs)
    id_wait.wait_recv()
    first = jnp.broadcast_to(id_in[:, 6:7, :], (devices, 8, 128))
    second = jnp.broadcast_to(id_in[:, 7:8, :], (devices, 8, 128))
    held = jnp.where((slot_of == 0)[None], first, second)
    wanted = jnp.where(matched, index + 1, -1).astype(F32)
    hot_c = jnp.where(held == wanted[None], 1.0, 0.0).astype(F32).reshape(devices * 8, 128)
    pick_c[:, 0:128] = hot_c.astype(BF16)
    pick_c[:, 128:256] = hot_c.astype(BF16)

    def send_flow(t, u):
        u_out[t] = spread(pick_c, flow_rows(u))
        exchange(u_out.at[t], u_in.at[t], 0, 6, u_ss.at[t], u_rs.at[t])

    def wait_flow(t):
        whole(u_out.at[t], u_in.at[t], 0, 6, u_ss.at[t], u_rs.at[t]).wait_recv()


    def send_weight(t, v):
        w_out[t] = spread(pick_h, weighted(v))
        exchange(w_out.at[t], w_in.at[t], 0, w_rows(t), w_ss.at[t], w_rs.at[t])

    def wait_weight(t):
        whole(w_out.at[t], w_in.at[t], 0, w_rows(t), w_ss.at[t], w_rs.at[t]).wait_recv()

    def advance(t, v, pushed):
        wait_flow(t)
        block = collect(pick_ht, u_in[t], True)
        updated = []
        for a in range(3):
            u = block[a * 32 : a * 32 + 32]
            updated.append(v[a] + rate * (u - v[a]) + pushed[a])
        return updated

    def halo_copy(t, first_out, tiles, first_in, px, py, pz):
        return pltpu.make_async_remote_copy(
            src_ref=halo_out.at[t, pl.ds(first_out, tiles)],
            dst_ref=halo_in.at[t, pl.ds(first_in, tiles)],
            send_sem=h_ss.at[t],
            recv_sem=h_rs.at[t],
            device_id=(px, py, pz),
            device_id_type=MESH,
        )

    def collide(t, read, flow, field):
        rho, speed = flow
        scale = 1.0 / (1.0 + 0.5 * field[3])
        force = [field[a] - field[3] * speed[a] for a in range(3)]
        target = [scale * (speed[a] + relax_time * force[a] / rho) for a in range(3)]
        square = target[0] * target[0] + target[1] * target[1] + target[2] * target[2]
        base = 1.0 - 1.5 * square
        for i in range(19):
            along = None
            for a in range(3):
                c = VELOCITIES[i][a]
                if c == 1:
                    along = target[a] if along is None else along + target[a]
                elif c == -1:
                    along = -target[a] if along is None else along - target[a]
            shape = base if along is None else base + along * (3.0 + 4.5 * along)
            f = read(i)
            post[pl.ds(i * 32, 32), :] = f - (f - WEIGHTS[i] * rho * shape) / relax_time

    def tile(i, x):
        return post[pl.ds(i * 32 + x * 8, 8), :]

    def send_halo(t):
        for n in range(5):
            halo_out[t, n] = tile(X_UP[n], 3)
            halo_out[t, 5 + n] = tile(X_DOWN[n], 0)
            half = pl.ds((n % 2) * 4, 4)
            halo_out[t, 10 + n // 2, half, :] = post[pl.ds(Y_UP[n] * 32 + 7, 4, stride=8), :]
            halo_out[t, 13 + n // 2, half, :] = post[pl.ds(Y_DOWN[n] * 32, 4, stride=8), :]
        halo_out[t, 12, 4:8, :] = jnp.zeros((4, 128), F32)
        halo_out[t, 15, 4:8, :] = jnp.zeros((4, 128), F32)
        packed = jnp.zeros((8, 128), F32)
        for n in range(5):
            for x in range(4):
                k = n * 4 + x
                up = pltpu.roll(tile(Z_UP[n], x), (k + 1) % 128, 1)
                down = pltpu.roll(tile(Z_DOWN[n], x), k, 1) if k else tile(Z_DOWN[n], x)
                packed = jnp.where(lane == k, jnp.where(gz == 0, up, down), packed)
        halo_out[t, 16] = packed
        halo_copy(t, 0, 5, 0, east, gy, gz).start()
        halo_copy(t, 5, 5, 5, west, gy, gz).start()
        halo_copy(t, 10, 3, 10, gx, north, gz).start()
        halo_copy(t, 13, 3, 13, gx, south, gz).start()
        halo_copy(t, 1, 1, 16, east, north, gz).start()
        halo_copy(t, 6, 1, 17, west, south, gz).start()
        halo_copy(t, 2, 1, 18, east, south, gz).start()
        halo_copy(t, 7, 1, 19, west, north, gz).start()
        for n, (px, py) in enumerate(across):
            halo_copy(t, 16, 1, 20 + n, px, py, beyond).start()

    def halo_whole(t):
        return pltpu.make_async_remote_copy(
            src_ref=halo_in.at[t],
            dst_ref=halo_in.at[t],
            send_sem=h_ss.at[t],
            recv_sem=h_rs.at[t],
            device_id=(gx, gy, beyond),
            device_id_type=MESH,
        )

    def stream(t, write):
        halo_whole(t).wait_recv()
        level = halo_in[t, 20]
        block_of = lane // 4
        from_west = pltpu.roll(halo_in[t, 21], 125, 1)
        from_east = pltpu.roll(halo_in[t, 22], 3, 1)
        right = jnp.where(lane % 4 == 0, from_west, pltpu.roll(level, 1, 1))
        left = jnp.where(lane % 4 == 3, from_east, pltpu.roll(level, 127, 1))
        upper = jnp.where(sub == 0, pltpu.roll(halo_in[t, 23], 1, 0), pltpu.roll(level, 1, 0))
        lower = jnp.where(sub == 7, pltpu.roll(halo_in[t, 24], 7, 0), pltpu.roll(level, 7, 0))
        ghost = jnp.where(block_of == 1, right, level)
        ghost = jnp.where(block_of == 2, left, ghost)
        ghost = jnp.where(block_of == 3, upper, ghost)
        ghost = jnp.where(block_of == 4, lower, ghost)

        for i in range(19):
            cx, cy, cz = VELOCITIES[i]
            for x in range(4):
                sx = x - cx
                inside = 0 <= sx < 4
                if inside:
                    value = tile(i, sx)
                elif cx == 1:
                    value = halo_in[t, X_UP.index(i)]
                else:
                    value = halo_in[t, 5 + X_DOWN.index(i)]
                if cy == 1:
                    n = Y_UP.index(i)
                    if inside:
                        row = jnp.broadcast_to(
                            halo_in[t, 10 + n // 2, pl.ds((n % 2) * 4 + sx, 1), :], (8, 128)
                        )
                    else:
                        row = jnp.broadcast_to(
                            halo_in[t, 16 if cx == 1 else 19, pl.ds(7, 1), :], (8, 128)
                        )
                    value = jnp.where(sub == 0, row, pltpu.roll(value, 1, 0))
                elif cy == -1:
                    n = Y_DOWN.index(i)
                    if inside:
                        row = jnp.broadcast_to(
                            halo_in[t, 13 + n // 2, pl.ds((n % 2) * 4 + sx, 1), :], (8, 128)
                        )
                    else:
                        row = jnp.broadcast_to(
                            halo_in[t, 18 if cx == 1 else 17, pl.ds(0, 1), :], (8, 128)
                        )
                    value = jnp.where(sub == 7, row, pltpu.roll(value, 7, 0))
                if cz != 0:
                    n = (Z_UP if cz == 1 else Z_DOWN).index(i)
                    k = n * 4 + x
                    edge = jnp.broadcast_to(ghost[:, k : k + 1], (8, 128))
                    wall = tile(OPPOSITE[i], x)
                    if cz == 1:
                        edge = jnp.where(gz == 1, edge, wall)
                        value = jnp.where(lane == 0, edge, pltpu.roll(value, 1, 1))
                    else:
                        edge = jnp.where(gz == 0, edge, wall)
                        value = jnp.where(lane == 127, edge, pltpu.roll(value, 127, 1))
                write(i, x, value)

    def write_next(i, x, value):
        fnow[pl.ds(i * 32 + x * 8, 8), :] = value

    def write_last(i, x, value):
        fluid[i, x] = value

    def fluid_step(t, read, flow, field, write):
        collide(t, read, flow, field)
        send_halo(t)
        stream(t, write)

    def field_of(t, before):
        wait_weight(t)
        table = collect(pick_ct, w_in[t], True)
        parts = [table[a * 32 : a * 32 + 32] + solid2 * before[a] for a in range(3)]
        return parts + [solid]

    send_flow(0, flow[1])
    pushed = contact_push(velocity)
    send_weight(1, without_flow(velocity, pushed))
    pick_ct[...] = hot_c.T.astype(BF16)

    wait_weight(0)
    table = collect(pick_ct, w_in[0], False)
    solid = table[96:128]
    field = [table[a * 32 : a * 32 + 32] for a in range(3)] + [solid]
    collide(0, read_first, flow, field)
    send_halo(0)
    tail = w_in[0].reshape(devices * 8, 128)
    tail = jnp.where(lax.broadcasted_iota(jnp.int32, (devices * 8, 128), 0) % 8 < 6, 0.0, tail)
    solid2 = collect(pick_ct, tail * tail, False)[96:128]
    stream(0, write_next)
    before = flow[1]
    flow = moments(read_next)
    send_flow(1, flow[1])

    velocity = advance(0, velocity, pushed)
    pushed = contact_push(velocity)
    send_weight(2, without_flow(velocity, pushed))

    fluid_step(1, read_next, flow, field_of(1, before), write_next)
    before = flow[1]
    flow = moments(read_next)
    send_flow(2, flow[1])

    velocity = advance(1, velocity, pushed)
    pushed = contact_push(velocity)
    send_weight(3, without_flow(velocity, pushed))

    fluid_step(2, read_next, flow, field_of(2, before), write_next)
    before = flow[1]
    flow = moments(read_next)
    send_flow(3, flow[1])

    velocity = advance(2, velocity, pushed)
    pushed = contact_push(velocity)

    fluid_step(3, read_next, flow, field_of(3, before), write_last)

    velocity = advance(3, velocity, pushed)
    for a in range(3):
        grains[a] = velocity[a]

    id_wait.wait_send()
    for t in range(SUBSTEPS):
        whole(u_out.at[t], u_in.at[t], 0, 6, u_ss.at[t], u_rs.at[t]).wait_send()
        whole(w_out.at[t], w_in.at[t], 0, w_rows(t), w_ss.at[t], w_rs.at[t]).wait_send()
        halo_whole(t).wait_send()


def solution(mesh):
    n_gx, n_gy = mesh.shape["gx"], mesh.shape["gy"]
    devices = n_gx * n_gy
    vmem = pl.BlockSpec(memory_space=pltpu.VMEM)
    smem = pl.BlockSpec(memory_space=pltpu.SMEM)
    dma = pltpu.SemaphoreType.DMA

    def body(populations, grain_velocity, grain_volume, slots, contacts, bin_cell):
        return pl.pallas_call(
            lambda *refs: kernel(n_gx, n_gy, *refs),
            out_shape=(
                jax.ShapeDtypeStruct(populations.shape, F32),
                jax.ShapeDtypeStruct(grain_velocity.shape, F32),
            ),
            in_specs=[vmem] * 5 + [smem],
            out_specs=(vmem, vmem),
            scratch_shapes=[
                pltpu.VMEM((608, 128), F32),
                pltpu.VMEM((608, 128), F32),
                pltpu.VMEM((devices * 8, 256), BF16),
                pltpu.VMEM((128, devices * 8), BF16),
                pltpu.VMEM((devices * 8, 256), BF16),
                pltpu.VMEM((128, devices * 8), BF16),
                pltpu.VMEM((devices, 8, 128), F32),
                pltpu.VMEM((devices, 8, 128), F32),
                pltpu.VMEM((SUBSTEPS, devices, 8, 128), F32),
                pltpu.VMEM((SUBSTEPS, devices, 8, 128), F32),
                pltpu.VMEM((SUBSTEPS, devices, 8, 128), F32),
                pltpu.VMEM((SUBSTEPS, devices, 8, 128), F32),
                pltpu.VMEM((SUBSTEPS, 17, 8, 128), F32),
                pltpu.VMEM((SUBSTEPS, 25, 8, 128), F32),
                dma,
                dma,
                dma((SUBSTEPS,)),
                dma((SUBSTEPS,)),
                dma((SUBSTEPS,)),
                dma((SUBSTEPS,)),
                dma((SUBSTEPS,)),
                dma((SUBSTEPS,)),
            ],
            compiler_params=pltpu.CompilerParams(
                collective_id=0, has_side_effects=True, vmem_limit_bytes=48 << 20
            ),
            name="bed",
        )(populations, grain_velocity, grain_volume, slots, contacts, bin_cell)

    every = ("gx", "gy", "gz")
    in_specs = (
        P(None, "gx", "gy", "gz"),
        P(None, every, None),
        P(every, None),
        P(every, None),
        P(every, None),
        P(every),
    )
    out_specs = (P(None, "gx", "gy", "gz"), P(None, every, None))
    return jax.shard_map(body, mesh=mesh, in_specs=in_specs, out_specs=out_specs, check_vma=False)
```

```python
import jax
import jax.numpy as jnp
import numpy as np
from jax import lax
from jax.experimental import pallas as pl
from jax.experimental.pallas import tpu as pltpu
from jax.sharding import PartitionSpec as P

SUBSTEPS = 4
VELOCITIES = [
    (0, 0, 0),
    (1, 0, 0), (-1, 0, 0), (0, 1, 0), (0, -1, 0), (0, 0, 1), (0, 0, -1),
    (1, 1, 0), (-1, -1, 0), (1, -1, 0), (-1, 1, 0),
    (1, 0, 1), (-1, 0, -1), (1, 0, -1), (-1, 0, 1),
    (0, 1, 1), (0, -1, -1), (0, 1, -1), (0, -1, 1),
]
WEIGHTS = [1.0 / 3.0] + [1.0 / 18.0] * 6 + [1.0 / 36.0] * 12
OPPOSITE = [0, 2, 1, 4, 3, 6, 5, 8, 7, 10, 9, 12, 11, 14, 13, 16, 15, 18, 17]
relax_time = 0.8
contact_stiffness = 0.1
drag_factor = 2.0
gravity = 0.01

X_UP = [1, 7, 9, 11, 13]
X_DOWN = [2, 8, 10, 12, 14]
Y_UP = [3, 7, 10, 15, 17]
Y_DOWN = [4, 8, 9, 16, 18]
Z_UP = [5, 11, 14, 15, 18]
Z_DOWN = [6, 13, 12, 17, 16]
SOURCE = [0, -1, 1, -2, 2, -3, 3, 4]
GROUPS = [(0, 1), (1, 4), (5, 3)]

F32 = jnp.float32
BF16 = jnp.bfloat16
MESH = pl.DeviceIdType.MESH


def split(x):
    high = x.astype(BF16)
    low = (x - high.astype(F32)).astype(BF16)
    return high, low


def kernel(
    n_gx, n_gy,
    pop, vel, vol, slots, contacts, cells,
    fluid, grains,
    post, fnow, pick_w, pick_u, pick_ht, pick_ct,
    idh_out, idh_in, idw_out, idw_in,
    u_raw, w_raw, u_out, u_in, w_out, w_in, halo_out, halo_in,
    idh_ss, idh_rs, idw_ss, idw_rs,
    u_zss, u_zrs, u_ss, u_rs, w_zss, w_zrs, w_ss, w_rs, h_ss, h_rs,
):
    n_z, n_c = 8, 2
    n_xh, n_y = n_gx // n_z, n_gy // n_c
    plane = n_xh * n_gy
    gx, gy, gz = lax.axis_index("gx"), lax.axis_index("gy"), lax.axis_index("gz")
    xh, zc, yc, cc = gx // n_z, gx % n_z, gy // n_c, gy % n_c
    me = xh * n_gy + gy

    def along_z(by):
        return (xh * n_z + (zc + by + n_z) % n_z, gy, gz)

    def in_plane(m):
        px = (xh + m // n_gy) % n_xh
        py = (yc + (m // n_c) % n_y) % n_y * n_c + (cc + m % n_c) % n_c
        return px, py

    west, east = (gx + n_gx - 1) % n_gx, (gx + 1) % n_gx
    south, north = (gy + n_gy - 1) % n_gy, (gy + 1) % n_gy
    beyond = 1 - gz
    across = [(gx, gy), (east, gy), (west, gy), (gx, north), (gx, south)]
    corners = [(east, north), (west, south), (east, south), (west, north)]

    barrier = pltpu.get_barrier_semaphore()
    greeted = [along_z(by) for by in (2, -2, 1, -1)]
    for m in range(plane - 1, 0, -1):
        px, py = in_plane(m)
        greeted.append((px * n_z + zc, py, gz))
    greeted += [(px, py, gz) for px, py in [(east, gy), (west, gy)] + corners]
    greeted += [(px, py, beyond) for px, py in across]
    for device in greeted:
        pl.semaphore_signal(barrier, inc=1, device_id=device, device_id_type=MESH)

    def z_copy(raw, t, source, region, by, start, rows, ss, rs, sem):
        part = pl.ds(start, rows)
        return pltpu.make_async_remote_copy(
            src_ref=raw.at[t, source, part],
            dst_ref=raw.at[t, region, part],
            send_sem=ss.at[t],
            recv_sem=rs.at[t, sem],
            device_id=along_z(by),
            device_id_type=MESH,
        )

    def plane_send(out, inn, ss, rs, first, tiles, row, rows):
        part = (pl.ds(first, tiles), pl.ds(row, rows))

        def send(i, carry):
            px, py = in_plane(plane - 1 - i)
            pltpu.make_async_remote_copy(
                src_ref=out.at[(px * n_gy + py,) + part],
                dst_ref=inn.at[(me,) + part],
                send_sem=ss,
                recv_sem=rs,
                device_id=(px * n_z + zc, py, gz),
                device_id_type=MESH,
            ).start()
            return carry

        lax.fori_loop(0, plane - 1, send, 0)
        inn[me, pl.ds(first, tiles)] = out[me, pl.ds(first, tiles)]

    def plane_whole(out, inn, ss, rs, first, tiles, row, rows):
        span = (pl.ds(0, plane - 1), pl.ds(first, tiles), pl.ds(row, rows))
        return pltpu.make_async_remote_copy(
            src_ref=out.at[span],
            dst_ref=inn.at[span],
            send_sem=ss,
            recv_sem=rs,
            device_id=(gx, gy, beyond),
            device_id_type=MESH,
        )

    sub = lax.broadcasted_iota(jnp.int32, (8, 128), 0)
    lane = lax.broadcasted_iota(jnp.int32, (8, 128), 1)
    matched = ((sub < 6) & (lane // 32 == sub % 3)) | ((sub >= 6) & (lane >= 96))
    slot_of = jnp.where(sub < 6, sub // 3, sub - 6)
    index = lane % 32

    cell = jnp.zeros((8, 128), jnp.int32)
    for b in range(32):
        cell = jnp.where(index == b, cells[b], cell)
    width = 8 * n_gy

    def source_of(c):
        column = c // 2
        return (column // width) // 4 * n_gy + (column % width) // 8

    source = source_of(cell)
    local = (cell // 2 // width) % 4 * 8 + (cell // 2 % width) % 8
    rank = jnp.zeros((8, 128), jnp.int32)
    for b in range(31):
        rank = rank + jnp.where((source == source_of(cells[b])) & (index > b), 1, 0)

    def placed(device):
        x, y = device // n_gy, device % n_gy
        return x // n_z * n_gy + y, x % n_z

    def hot_ids(hot, column):
        return jnp.sum(hot * column, axis=-1, keepdims=True)

    side, depth = placed(source)
    away = (depth - zc + n_z) % n_z
    region_of = jnp.zeros((8, 128), jnp.int32)
    for r, by in enumerate(SOURCE):
        region_of = jnp.where(away == by % n_z, r, region_of)
    code = jnp.where(matched, 2 * (side * n_z + region_of) + rank - slot_of, -1000000)
    target = lax.broadcasted_iota(jnp.int32, (plane * n_z, 8, 128), 0) * 2
    hot_h = jnp.where(code[None] == target, 1.0, 0.0).astype(F32)
    column = (local + 1).astype(F32)
    idh_out[...] = jnp.broadcast_to(
        hot_ids(hot_h, column[None]), (plane * n_z, 8, 128)
    ).reshape(plane, n_z, 8, 128)

    def spread(pick, table):
        if table.shape[0] == 96:
            table = jnp.concatenate([table, jnp.zeros((32, 128), F32)], axis=0)
        high, low = split(table)
        both = jnp.concatenate([high, low], axis=0)
        rows = jnp.dot(pick, both, preferred_element_type=F32)
        return rows.reshape(plane, 8, 128)

    def collect(pick_t, rows, masked):
        if masked:
            inside = lax.broadcasted_iota(jnp.int32, rows.shape, 0) % 8 < 6
            rows = jnp.where(inside, rows, 0.0)
        high, low = split(rows)
        table = pick_t[...]
        return jnp.dot(table, high, preferred_element_type=F32) + jnp.dot(
            table, low, preferred_element_type=F32
        )

    def flat(tiles):
        return tiles.reshape(plane * n_z * 8, 128)

    live = slots[...].astype(F32)
    rate = drag_factor * vol[...] * live
    links = contacts[...].astype(F32).astype(BF16)
    count = jnp.dot(links, live.astype(BF16), preferred_element_type=F32)

    def near(moving):
        high, low = split(moving)
        return jnp.dot(links, high, preferred_element_type=F32) + jnp.dot(
            links, low, preferred_element_type=F32
        )

    def contact_push(v):
        pushed = []
        for a in range(3):
            push = contact_stiffness * live * (near(v[a] * live) - count * v[a])
            pushed.append(push - gravity * live if a == 2 else push)
        return pushed

    velocity = [vel[a] for a in range(3)]
    for a in range(3):
        w_raw[0, 0, a * 32 : a * 32 + 32, :] = rate * velocity[a]
    w_raw[0, 0, 96:128, :] = rate
    w_raw[0, 0, 128:136, :] = jnp.where(sub == 0, 2 * source + rank, local + 1).astype(F32)

    def moments(read):
        rho = jnp.zeros((32, 128), F32)
        momentum = [jnp.zeros((32, 128), F32) for _ in range(3)]
        for i in range(19):
            f = read(i)
            rho = rho + f
            for a in range(3):
                if VELOCITIES[i][a] == 1:
                    momentum[a] = momentum[a] + f
                elif VELOCITIES[i][a] == -1:
                    momentum[a] = momentum[a] - f
        return rho, [m / rho for m in momentum]

    read_first = lambda i: pop[i].reshape(32, 128)
    read_next = lambda i: fnow[pl.ds(i * 32, 32), :]
    flow = moments(read_first)

    class Exchange:
        def __init__(self, raw, out, inn, zss, zrs, ss, rs, t, rows, shown, spread_one):
            self.raw, self.out, self.inn, self.t = raw, out, inn, t
            self.z_sems, self.p_sems = (zss, zrs), (ss.at[t], rs)
            self.rows, self.shown, self.spread_one = rows, shown, spread_one
            self.half = rows // 16 * 8

        def z(self, source, region, by, start=0, rows=None, sem=None):
            rows = self.rows if rows is None else rows
            sem = region if sem is None else sem
            return z_copy(self.raw, self.t, source, region, by, start, rows, *self.z_sems, sem)

        def start(self):
            for by, region in ((2, 3), (-2, 4), (1, 1), (-1, 2)):
                self.z(0, region, by).start()

        def got(self, region):
            self.z(region, region, 1).wait_recv()

        def send(self, g):
            first, tiles = GROUPS[g]
            for r in range(first, first + tiles):
                self.spread_one(self.t, r)
            plane_send(
                self.out.at[self.t], self.inn.at[self.t], self.p_sems[0],
                self.p_sems[1].at[self.t, g], first, tiles, 0, self.shown,
            )

        def forward(self):
            self.got(3)
            self.z(3, 7, 2, 0, self.half, 7).start()
            self.z(3, 5, 1).start()
            self.got(4)
            self.z(4, 7, -2, self.half, self.rows - self.half, 8).start()
            self.z(4, 6, -1).start()

        def near_parts(self):
            self.got(1)
            self.got(2)
            self.send(1)

        def far_parts(self):
            self.got(5)
            self.got(6)
            self.z(7, 7, 1, 0, self.half, 7).wait_recv()
            self.z(7, 7, 1, self.half, self.rows - self.half, 8).wait_recv()
            self.send(2)

        def whole(self, g, first, tiles):
            return plane_whole(
                self.out.at[self.t], self.inn.at[self.t], self.p_sems[0],
                self.p_sems[1].at[self.t, g], first, tiles, 0, self.shown,
            )

        def receive(self):
            for g in range(3):
                self.whole(g, *GROUPS[g]).wait_recv()
            return flat(self.inn[self.t])

        def finish(self):
            part = (self.t, pl.ds(0, 7), pl.ds(0, self.rows))
            pltpu.make_async_remote_copy(
                src_ref=self.raw.at[part],
                dst_ref=self.raw.at[part],
                send_sem=self.z_sems[0].at[self.t],
                recv_sem=self.z_sems[1].at[self.t, 0],
                device_id=along_z(1),
                device_id_type=MESH,
            ).wait_send()
            self.whole(0, 0, n_z).wait_send()

    def spread_flow(t, r):
        u_out[t, :, r] = spread(pick_u[r], u_raw[t, r])

    def spread_weight(t, r):
        w_out[t, :, r] = spread(pick_w[r], w_raw[t, r, 0:96, :])

    plane_target = lax.broadcasted_iota(jnp.int32, (plane, 8, 128), 0) * 2

    def spread_first(t, r):
        coded = jnp.broadcast_to(w_raw[0, r, 128:129, :], (8, 128)).astype(jnp.int32)
        lies, level = placed(coded // 2)
        wanted = jnp.where(
            matched & (level == zc), 2 * lies + coded % 2 - slot_of, -1000000
        )
        hot = jnp.where(wanted[None] == plane_target, 1.0, 0.0).astype(F32)
        where_to = jnp.broadcast_to(w_raw[0, r, 129:130, :], (8, 128))
        idw_out[:, r] = jnp.broadcast_to(hot_ids(hot, where_to[None]), (plane, 8, 128))
        hot = hot.reshape(plane * 8, 128).astype(BF16)
        pick_w[r, :, 0:128] = hot
        pick_w[r, :, 128:256] = hot
        w_out[0, :, r] = spread(pick_w[r], w_raw[0, r, 0:128, :])

    weights = [
        Exchange(
            w_raw, w_out, w_in, w_zss, w_zrs, w_ss, w_rs, t,
            136 if t == 0 else 96, 8 if t == 0 else 6, spread_first if t == 0 else spread_weight,
        )
        for t in range(SUBSTEPS)
    ]
    flows = [
        Exchange(u_raw, u_out, u_in, u_zss, u_zrs, u_ss, u_rs, t, 96, 6, spread_flow)
        for t in range(SUBSTEPS)
    ]

    def send_ids(g):
        plane_send(idw_out, idw_in, idw_ss, idw_rs.at[g], *GROUPS[g], 6, 2)

    def picked(id_tiles):
        first = jnp.broadcast_to(id_tiles[:, 6:7, :], id_tiles.shape)
        second = jnp.broadcast_to(id_tiles[:, 7:8, :], id_tiles.shape)
        held = jnp.where((slot_of == 0)[None], first, second)
        wanted = jnp.where(matched, index + 1, -1).astype(F32)
        return jnp.where(held == wanted[None], 1.0, 0.0).astype(F32)

    def start_flow(t, u):
        for a in range(3):
            u_raw[t, 0, a * 32 : a * 32 + 32, :] = u[a]
        flows[t].start()

    def start_weight(t, v, pushed):
        for a in range(3):
            w_raw[t, 0, a * 32 : a * 32 + 32, :] = rate * ((1.0 - rate) * v[a] + pushed[a])
        weights[t].start()
        weights[t].send(0)

    def advance(t, v, pushed):
        block = collect(pick_ht, flows[t].receive(), True)
        updated = []
        for a in range(3):
            u = block[a * 32 : a * 32 + 32]
            updated.append(v[a] + rate * (u - v[a]) + pushed[a])
        return updated

    def halo_copy(t, first_out, tiles, first_in, px, py, pz):
        return pltpu.make_async_remote_copy(
            src_ref=halo_out.at[t, pl.ds(first_out, tiles)],
            dst_ref=halo_in.at[t, pl.ds(first_in, tiles)],
            send_sem=h_ss.at[t],
            recv_sem=h_rs.at[t],
            device_id=(px, py, pz),
            device_id_type=MESH,
        )

    def collide(t, read, flow, field):
        rho, speed = flow
        scale = 1.0 / (1.0 + 0.5 * field[3])
        force = [field[a] - field[3] * speed[a] for a in range(3)]
        target = [scale * (speed[a] + relax_time * force[a] / rho) for a in range(3)]
        square = target[0] * target[0] + target[1] * target[1] + target[2] * target[2]
        base = 1.0 - 1.5 * square
        for i in range(19):
            along = None
            for a in range(3):
                c = VELOCITIES[i][a]
                if c == 1:
                    along = target[a] if along is None else along + target[a]
                elif c == -1:
                    along = -target[a] if along is None else along - target[a]
            shape = base if along is None else base + along * (3.0 + 4.5 * along)
            f = read(i)
            post[pl.ds(i * 32, 32), :] = f - (f - WEIGHTS[i] * rho * shape) / relax_time

    def tile(i, x):
        return post[pl.ds(i * 32 + x * 8, 8), :]

    def send_halo(t):
        for n in range(5):
            halo_out[t, n] = tile(X_UP[n], 3)
            halo_out[t, 5 + n] = tile(X_DOWN[n], 0)
            half = pl.ds((n % 2) * 4, 4)
            halo_out[t, 10 + n // 2, half, :] = post[pl.ds(Y_UP[n] * 32 + 7, 4, stride=8), :]
            halo_out[t, 13 + n // 2, half, :] = post[pl.ds(Y_DOWN[n] * 32, 4, stride=8), :]
        halo_out[t, 12, 4:8, :] = jnp.zeros((4, 128), F32)
        halo_out[t, 15, 4:8, :] = jnp.zeros((4, 128), F32)
        packed = jnp.zeros((8, 128), F32)
        for n in range(5):
            for x in range(4):
                k = n * 4 + x
                up = pltpu.roll(tile(Z_UP[n], x), (k + 1) % 128, 1)
                down = pltpu.roll(tile(Z_DOWN[n], x), k, 1) if k else tile(Z_DOWN[n], x)
                packed = jnp.where(lane == k, jnp.where(gz == 0, up, down), packed)
        halo_out[t, 16] = packed
        halo_copy(t, 0, 5, 0, east, gy, gz).start()
        halo_copy(t, 5, 5, 5, west, gy, gz).start()
        halo_copy(t, 10, 3, 10, gx, north, gz).start()
        halo_copy(t, 13, 3, 13, gx, south, gz).start()
        halo_copy(t, 1, 1, 16, east, north, gz).start()
        halo_copy(t, 6, 1, 17, west, south, gz).start()
        halo_copy(t, 2, 1, 18, east, south, gz).start()
        halo_copy(t, 7, 1, 19, west, north, gz).start()
        for n, (px, py) in enumerate(across):
            halo_copy(t, 16, 1, 20 + n, px, py, beyond).start()

    def halo_whole(t):
        return pltpu.make_async_remote_copy(
            src_ref=halo_in.at[t],
            dst_ref=halo_in.at[t],
            send_sem=h_ss.at[t],
            recv_sem=h_rs.at[t],
            device_id=(gx, gy, beyond),
            device_id_type=MESH,
        )

    def stream(t, write):
        halo_whole(t).wait_recv()
        level = halo_in[t, 20]
        block_of = lane // 4
        from_west = pltpu.roll(halo_in[t, 21], 125, 1)
        from_east = pltpu.roll(halo_in[t, 22], 3, 1)
        right = jnp.where(lane % 4 == 0, from_west, pltpu.roll(level, 1, 1))
        left = jnp.where(lane % 4 == 3, from_east, pltpu.roll(level, 127, 1))
        upper = jnp.where(sub == 0, pltpu.roll(halo_in[t, 23], 1, 0), pltpu.roll(level, 1, 0))
        lower = jnp.where(sub == 7, pltpu.roll(halo_in[t, 24], 7, 0), pltpu.roll(level, 7, 0))
        ghost = jnp.where(block_of == 1, right, level)
        ghost = jnp.where(block_of == 2, left, ghost)
        ghost = jnp.where(block_of == 3, upper, ghost)
        ghost = jnp.where(block_of == 4, lower, ghost)

        for i in range(19):
            cx, cy, cz = VELOCITIES[i]
            for x in range(4):
                sx = x - cx
                inside = 0 <= sx < 4
                if inside:
                    value = tile(i, sx)
                elif cx == 1:
                    value = halo_in[t, X_UP.index(i)]
                else:
                    value = halo_in[t, 5 + X_DOWN.index(i)]
                if cy == 1:
                    n = Y_UP.index(i)
                    if inside:
                        row = jnp.broadcast_to(
                            halo_in[t, 10 + n // 2, pl.ds((n % 2) * 4 + sx, 1), :], (8, 128)
                        )
                    else:
                        row = jnp.broadcast_to(
                            halo_in[t, 16 if cx == 1 else 19, pl.ds(7, 1), :], (8, 128)
                        )
                    value = jnp.where(sub == 0, row, pltpu.roll(value, 1, 0))
                elif cy == -1:
                    n = Y_DOWN.index(i)
                    if inside:
                        row = jnp.broadcast_to(
                            halo_in[t, 13 + n // 2, pl.ds((n % 2) * 4 + sx, 1), :], (8, 128)
                        )
                    else:
                        row = jnp.broadcast_to(
                            halo_in[t, 18 if cx == 1 else 17, pl.ds(0, 1), :], (8, 128)
                        )
                    value = jnp.where(sub == 7, row, pltpu.roll(value, 7, 0))
                if cz != 0:
                    n = (Z_UP if cz == 1 else Z_DOWN).index(i)
                    k = n * 4 + x
                    edge = jnp.broadcast_to(ghost[:, k : k + 1], (8, 128))
                    wall = tile(OPPOSITE[i], x)
                    if cz == 1:
                        edge = jnp.where(gz == 1, edge, wall)
                        value = jnp.where(lane == 0, edge, pltpu.roll(value, 1, 1))
                    else:
                        edge = jnp.where(gz == 0, edge, wall)
                        value = jnp.where(lane == 127, edge, pltpu.roll(value, 127, 1))
                write(i, x, value)

    def write_next(i, x, value):
        fnow[pl.ds(i * 32 + x * 8, 8), :] = value

    def write_last(i, x, value):
        fluid[i, x] = value

    def field_of(t, before):
        table = collect(pick_ct, weights[t].receive(), True)
        parts = [table[a * 32 : a * 32 + 32] + solid2 * before[a] for a in range(3)]
        return parts + [solid]

    pl.semaphore_wait(barrier, len(greeted))
    weights[0].start()
    plane_send(idh_out, idh_in, idh_ss, idh_rs, 0, n_z, 6, 2)
    weights[0].send(0)
    send_ids(0)
    pick_ht[...] = flat(hot_h).T.astype(BF16)
    pushed = contact_push(velocity)

    weights[0].forward()
    start_flow(0, flow[1])
    weights[0].near_parts()
    send_ids(1)

    idh_whole = plane_whole(idh_out, idh_in, idh_ss, idh_rs, 0, n_z, 6, 2)
    idh_whole.wait_recv()
    for r in range(n_z):
        hot = picked(idh_in[:, r]).reshape(plane * 8, 128).astype(BF16)
        pick_u[r, :, 0:128] = hot
        pick_u[r, :, 128:256] = hot
    flows[0].send(0)
    weights[0].far_parts()
    send_ids(2)

    flows[0].forward()
    start_weight(1, velocity, pushed)
    flows[0].near_parts()

    for g in range(3):
        plane_whole(idw_out, idw_in, idw_ss, idw_rs.at[g], *GROUPS[g], 6, 2).wait_recv()
    hot_c = picked(idw_in[...].reshape(plane * n_z, 8, 128))
    pick_ct[...] = flat(hot_c).T.astype(BF16)
    table = weights[0].receive()
    tail = jnp.where(lax.broadcasted_iota(jnp.int32, table.shape, 0) % 8 < 6, 0.0, table)
    table = collect(pick_ct, table, False)
    solid = table[96:128]
    field = [table[a * 32 : a * 32 + 32] for a in range(3)] + [solid]
    collide(0, read_first, flow, field)
    send_halo(0)
    flows[0].far_parts()
    weights[1].forward()
    solid2 = collect(pick_ct, tail * tail, False)[96:128]
    stream(0, write_next)
    before = flow[1]
    flow = moments(read_next)
    start_flow(1, flow[1])
    flows[1].send(0)

    velocity = advance(0, velocity, pushed)
    pushed = contact_push(velocity)
    start_weight(2, velocity, pushed)
    weights[1].near_parts()
    weights[1].far_parts()
    flows[1].forward()
    collide(1, read_next, flow, field_of(1, before))
    send_halo(1)
    flows[1].near_parts()
    weights[2].forward()
    stream(1, write_next)
    before = flow[1]
    flow = moments(read_next)
    start_flow(2, flow[1])
    flows[2].send(0)
    flows[1].far_parts()
    weights[2].near_parts()

    velocity = advance(1, velocity, pushed)
    pushed = contact_push(velocity)
    start_weight(3, velocity, pushed)
    weights[2].far_parts()
    flows[2].forward()
    collide(2, read_next, flow, field_of(2, before))
    send_halo(2)
    flows[2].near_parts()
    weights[3].forward()
    stream(2, write_next)
    before = flow[1]
    flow = moments(read_next)
    start_flow(3, flow[1])
    flows[3].send(0)
    weights[3].near_parts()
    flows[2].far_parts()
    weights[3].far_parts()
    flows[3].forward()
    flows[3].near_parts()

    velocity = advance(2, velocity, pushed)
    pushed = contact_push(velocity)
    collide(3, read_next, flow, field_of(3, before))
    send_halo(3)
    flows[3].far_parts()
    stream(3, write_last)

    velocity = advance(3, velocity, pushed)
    for a in range(3):
        grains[a] = velocity[a]

    idh_whole.wait_send()
    plane_whole(idw_out, idw_in, idw_ss, idw_rs.at[0], 0, n_z, 6, 2).wait_send()
    for t in range(SUBSTEPS):
        weights[t].finish()
        flows[t].finish()
        halo_whole(t).wait_send()


def solution(mesh):
    n_gx, n_gy = mesh.shape["gx"], mesh.shape["gy"]
    plane = n_gx // 8 * n_gy
    vmem = pl.BlockSpec(memory_space=pltpu.VMEM)
    smem = pl.BlockSpec(memory_space=pltpu.SMEM)
    dma = pltpu.SemaphoreType.DMA

    def body(populations, grain_velocity, grain_volume, slots, contacts, bin_cell):
        return pl.pallas_call(
            lambda *refs: kernel(n_gx, n_gy, *refs),
            out_shape=(
                jax.ShapeDtypeStruct(populations.shape, F32),
                jax.ShapeDtypeStruct(grain_velocity.shape, F32),
            ),
            in_specs=[vmem] * 5 + [smem],
            out_specs=(vmem, vmem),
            scratch_shapes=[
                pltpu.VMEM((608, 128), F32),
                pltpu.VMEM((608, 128), F32),
                pltpu.VMEM((8, plane * 8, 256), BF16),
                pltpu.VMEM((8, plane * 8, 256), BF16),
                pltpu.VMEM((128, plane * 64), BF16),
                pltpu.VMEM((128, plane * 64), BF16),
            ]
            + [pltpu.VMEM((plane, 8, 8, 128), F32)] * 4
            + [
                pltpu.VMEM((SUBSTEPS, 8, 96, 128), F32),
                pltpu.VMEM((SUBSTEPS, 8, 136, 128), F32),
            ]
            + [pltpu.VMEM((SUBSTEPS, plane, 8, 8, 128), F32)] * 4
            + [
                pltpu.VMEM((SUBSTEPS, 17, 8, 128), F32),
                pltpu.VMEM((SUBSTEPS, 25, 8, 128), F32),
                dma,
                dma,
                dma,
                dma((3,)),
            ]
            + [dma((SUBSTEPS,)), dma((SUBSTEPS, 9)), dma((SUBSTEPS,)), dma((SUBSTEPS, 3))] * 2
            + [dma((SUBSTEPS,)), dma((SUBSTEPS,))],
            compiler_params=pltpu.CompilerParams(
                collective_id=0, has_side_effects=True, vmem_limit_bytes=48 << 20
            ),
            name="bed",
        )(populations, grain_velocity, grain_volume, slots, contacts, bin_cell)

    every = ("gx", "gy", "gz")
    in_specs = (
        P(None, "gx", "gy", "gz"),
        P(None, every, None),
        P(every, None),
        P(every, None),
        P(every, None),
        P(every),
    )
    out_specs = (P(None, "gx", "gy", "gz"), P(None, every, None))
    return jax.shard_map(body, mesh=mesh, in_specs=in_specs, out_specs=out_specs, check_vma=False)
```

```python
import jax
import jax.numpy as jnp
import numpy as np
from jax import lax
from jax.experimental import pallas as pl
from jax.experimental.pallas import tpu as pltpu
from jax.sharding import PartitionSpec as P

SUBSTEPS = 4
VELOCITIES = [
    (0, 0, 0),
    (1, 0, 0), (-1, 0, 0), (0, 1, 0), (0, -1, 0), (0, 0, 1), (0, 0, -1),
    (1, 1, 0), (-1, -1, 0), (1, -1, 0), (-1, 1, 0),
    (1, 0, 1), (-1, 0, -1), (1, 0, -1), (-1, 0, 1),
    (0, 1, 1), (0, -1, -1), (0, 1, -1), (0, -1, 1),
]
WEIGHTS = [1.0 / 3.0] + [1.0 / 18.0] * 6 + [1.0 / 36.0] * 12
OPPOSITE = [0, 2, 1, 4, 3, 6, 5, 8, 7, 10, 9, 12, 11, 14, 13, 16, 15, 18, 17]
relax_time = 0.8
contact_stiffness = 0.1
drag_factor = 2.0
gravity = 0.01

X_UP = [1, 7, 9, 11, 13]
X_DOWN = [2, 8, 10, 12, 14]
Y_UP = [3, 7, 10, 15, 17]
Y_DOWN = [4, 8, 9, 16, 18]
Z_UP = [5, 11, 14, 15, 18]
Z_DOWN = [6, 13, 12, 17, 16]
SOURCE = [0, -1, 1, -2, 2, -3, 3, 4]
GROUPS = [(0, 1), (1, 4), (5, 3)]

ORDER = [
    "start_w0", "own_w0", "pick_h", "on_w0", "pick_u", "start_u0", "start_w1",
    "near_w0", "far_w0", "own_u0", "own_w1", "on_u0", "near_u0", "on_w1",
    "far_u0", "near_w1", "pick_c", "collide0", "far_w1", "grain0", "squares",
    "stream0", "collide1", "own_w2", "on_w2", "own_u1", "near_w2", "on_u1",
    "near_u1", "stream1", "far_w2", "far_u1", "own_u2", "on_u2", "collide2",
    "grain1", "near_u2", "own_w3", "on_w3", "stream2", "near_w3", "far_w3",
    "far_u2", "on_u3", "near_u3", "own_u3", "far_u3", "collide3", "grain2",
    "grain3", "stream3",
]

F32 = jnp.float32
BF16 = jnp.bfloat16
MESH = pl.DeviceIdType.MESH


def split(x):
    high = x.astype(BF16)
    low = (x - high.astype(F32)).astype(BF16)
    return high, low


def kernel(
    n_gx, n_gy,
    pop, vel, vol, slots, contacts, cells,
    fluid, grains,
    post, fnow, pick_w, pick_u, pick_ht, pick_ct,
    idh_out, idh_in, idw_out, idw_in,
    u_raw, w_raw, u_out, u_in, w_out, w_in, halo_out, halo_in,
    idh_ss, idh_rs, idw_ss, idw_rs,
    u_zss, u_zrs, u_ss, u_rs, w_zss, w_zrs, w_ss, w_rs, h_ss, h_rs,
):
    n_z, n_c = 8, 2
    n_xh, n_y = n_gx // n_z, n_gy // n_c
    plane = n_xh * n_gy
    gx, gy, gz = lax.axis_index("gx"), lax.axis_index("gy"), lax.axis_index("gz")
    xh, zc, yc, cc = gx // n_z, gx % n_z, gy // n_c, gy % n_c
    me = xh * n_gy + gy

    def along_z(by):
        return (xh * n_z + (zc + by + n_z) % n_z, gy, gz)

    def in_plane(m):
        px = (xh + m // n_gy) % n_xh
        py = (yc + (m // n_c) % n_y) % n_y * n_c + (cc + m % n_c) % n_c
        return px, py

    west, east = (gx + n_gx - 1) % n_gx, (gx + 1) % n_gx
    south, north = (gy + n_gy - 1) % n_gy, (gy + 1) % n_gy
    beyond = 1 - gz
    across = [(gx, gy), (east, gy), (west, gy), (gx, north), (gx, south)]
    corners = [(east, north), (west, south), (east, south), (west, north)]

    barrier = pltpu.get_barrier_semaphore()
    greeted = [along_z(by) for by in (2, -2, 1, -1)]
    for m in range(plane - 1, 0, -1):
        px, py = in_plane(m)
        greeted.append((px * n_z + zc, py, gz))
    greeted += [(px, py, gz) for px, py in [(east, gy), (west, gy)] + corners]
    greeted += [(px, py, beyond) for px, py in across]
    for device in greeted:
        pl.semaphore_signal(barrier, inc=1, device_id=device, device_id_type=MESH)

    def z_copy(raw, t, source, region, by, start, rows, ss, rs, sem):
        part = pl.ds(start, rows)
        return pltpu.make_async_remote_copy(
            src_ref=raw.at[t, source, part],
            dst_ref=raw.at[t, region, part],
            send_sem=ss.at[t],
            recv_sem=rs.at[t, sem],
            device_id=along_z(by),
            device_id_type=MESH,
        )

    def plane_send(out, inn, ss, rs, first, tiles, row, rows):
        part = (pl.ds(first, tiles), pl.ds(row, rows))

        def send(i, carry):
            px, py = in_plane(plane - 1 - i)
            pltpu.make_async_remote_copy(
                src_ref=out.at[(px * n_gy + py,) + part],
                dst_ref=inn.at[(me,) + part],
                send_sem=ss,
                recv_sem=rs,
                device_id=(px * n_z + zc, py, gz),
                device_id_type=MESH,
            ).start()
            return carry

        lax.fori_loop(0, plane - 1, send, 0)
        inn[me, pl.ds(first, tiles)] = out[me, pl.ds(first, tiles)]

    def plane_whole(out, inn, ss, rs, first, tiles, row, rows):
        span = (pl.ds(0, plane - 1), pl.ds(first, tiles), pl.ds(row, rows))
        return pltpu.make_async_remote_copy(
            src_ref=out.at[span],
            dst_ref=inn.at[span],
            send_sem=ss,
            recv_sem=rs,
            device_id=(gx, gy, beyond),
            device_id_type=MESH,
        )

    sub = lax.broadcasted_iota(jnp.int32, (8, 128), 0)
    lane = lax.broadcasted_iota(jnp.int32, (8, 128), 1)
    matched = ((sub < 6) & (lane // 32 == sub % 3)) | ((sub >= 6) & (lane >= 96))
    slot_of = jnp.where(sub < 6, sub // 3, sub - 6)
    index = lane % 32

    cell = jnp.zeros((8, 128), jnp.int32)
    for b in range(32):
        cell = jnp.where(index == b, cells[b], cell)
    width = 8 * n_gy

    def source_of(c):
        column = c // 2
        return (column // width) // 4 * n_gy + (column % width) // 8

    source = source_of(cell)
    local = (cell // 2 // width) % 4 * 8 + (cell // 2 % width) % 8
    rank = jnp.zeros((8, 128), jnp.int32)
    for b in range(31):
        rank = rank + jnp.where((source == source_of(cells[b])) & (index > b), 1, 0)

    def placed(device):
        x, y = device // n_gy, device % n_gy
        return x // n_z * n_gy + y, x % n_z

    def hot_ids(hot, column):
        return jnp.sum(hot * column, axis=-1, keepdims=True)

    side, depth = placed(source)
    away = (depth - zc + n_z) % n_z
    region_of = jnp.zeros((8, 128), jnp.int32)
    for r, by in enumerate(SOURCE):
        region_of = jnp.where(away == by % n_z, r, region_of)
    code = jnp.where(matched, 2 * (side * n_z + region_of) + rank - slot_of, -1000000)
    target = lax.broadcasted_iota(jnp.int32, (plane * n_z, 8, 128), 0) * 2
    hot_h = jnp.where(code[None] == target, 1.0, 0.0).astype(F32)
    column = (local + 1).astype(F32)
    idh_out[...] = jnp.broadcast_to(
        hot_ids(hot_h, column[None]), (plane * n_z, 8, 128)
    ).reshape(plane, n_z, 8, 128)

    def spread(pick, table):
        if table.shape[0] == 96:
            table = jnp.concatenate([table, jnp.zeros((32, 128), F32)], axis=0)
        high, low = split(table)
        both = jnp.concatenate([high, low], axis=0)
        rows = jnp.dot(pick, both, preferred_element_type=F32)
        return rows.reshape(plane, 8, 128)

    def collect(pick_t, rows, masked):
        if masked:
            inside = lax.broadcasted_iota(jnp.int32, rows.shape, 0) % 8 < 6
            rows = jnp.where(inside, rows, 0.0)
        high, low = split(rows)
        table = pick_t[...]
        return jnp.dot(table, high, preferred_element_type=F32) + jnp.dot(
            table, low, preferred_element_type=F32
        )

    def flat(tiles):
        return tiles.reshape(plane * n_z * 8, 128)

    live = slots[...].astype(F32)
    rate = drag_factor * vol[...] * live
    links = contacts[...].astype(F32).astype(BF16)
    count = jnp.dot(links, live.astype(BF16), preferred_element_type=F32)

    def near(moving):
        high, low = split(moving)
        return jnp.dot(links, high, preferred_element_type=F32) + jnp.dot(
            links, low, preferred_element_type=F32
        )

    def contact_push(v):
        pushed = []
        for a in range(3):
            push = contact_stiffness * live * (near(v[a] * live) - count * v[a])
            pushed.append(push - gravity * live if a == 2 else push)
        return pushed

    velocity = [vel[a] for a in range(3)]
    for a in range(3):
        w_raw[0, 0, a * 32 : a * 32 + 32, :] = rate * velocity[a]
    w_raw[0, 0, 96:128, :] = rate
    w_raw[0, 0, 128:136, :] = jnp.where(sub == 0, 2 * source + rank, local + 1).astype(F32)

    def moments(read):
        rho = jnp.zeros((32, 128), F32)
        momentum = [jnp.zeros((32, 128), F32) for _ in range(3)]
        for i in range(19):
            f = read(i)
            rho = rho + f
            for a in range(3):
                if VELOCITIES[i][a] == 1:
                    momentum[a] = momentum[a] + f
                elif VELOCITIES[i][a] == -1:
                    momentum[a] = momentum[a] - f
        return rho, [m / rho for m in momentum]

    read_first = lambda i: pop[i].reshape(32, 128)
    read_next = lambda i: fnow[pl.ds(i * 32, 32), :]
    flow = moments(read_first)

    class Exchange:
        def __init__(self, raw, out, inn, zss, zrs, ss, rs, t, rows, shown, spread_one):
            self.raw, self.out, self.inn, self.t = raw, out, inn, t
            self.z_sems, self.p_sems = (zss, zrs), (ss.at[t], rs)
            self.rows, self.shown, self.spread_one = rows, shown, spread_one
            self.half = rows // 16 * 8

        def z(self, source, region, by, start=0, rows=None, sem=None):
            rows = self.rows if rows is None else rows
            sem = region if sem is None else sem
            return z_copy(self.raw, self.t, source, region, by, start, rows, *self.z_sems, sem)

        def start(self):
            for by, region in ((2, 3), (-2, 4), (1, 1), (-1, 2)):
                self.z(0, region, by).start()

        def got(self, region):
            self.z(region, region, 1).wait_recv()

        def send(self, g):
            first, tiles = GROUPS[g]
            for r in range(first, first + tiles):
                self.spread_one(self.t, r)
            plane_send(
                self.out.at[self.t], self.inn.at[self.t], self.p_sems[0],
                self.p_sems[1].at[self.t, g], first, tiles, 0, self.shown,
            )

        def forward(self):
            self.got(3)
            self.z(3, 7, 2, 0, self.half, 7).start()
            self.z(3, 5, 1).start()
            self.got(4)
            self.z(4, 7, -2, self.half, self.rows - self.half, 8).start()
            self.z(4, 6, -1).start()

        def near_parts(self):
            self.got(1)
            self.got(2)
            self.send(1)

        def far_parts(self):
            self.got(5)
            self.got(6)
            self.z(7, 7, 1, 0, self.half, 7).wait_recv()
            self.z(7, 7, 1, self.half, self.rows - self.half, 8).wait_recv()
            self.send(2)

        def whole(self, g, first, tiles):
            return plane_whole(
                self.out.at[self.t], self.inn.at[self.t], self.p_sems[0],
                self.p_sems[1].at[self.t, g], first, tiles, 0, self.shown,
            )

        def receive(self):
            for g in range(3):
                self.whole(g, *GROUPS[g]).wait_recv()
            return flat(self.inn[self.t])

        def finish(self):
            part = (self.t, pl.ds(0, 7), pl.ds(0, self.rows))
            pltpu.make_async_remote_copy(
                src_ref=self.raw.at[part],
                dst_ref=self.raw.at[part],
                send_sem=self.z_sems[0].at[self.t],
                recv_sem=self.z_sems[1].at[self.t, 0],
                device_id=along_z(1),
                device_id_type=MESH,
            ).wait_send()
            self.whole(0, 0, n_z).wait_send()

    def spread_flow(t, r):
        u_out[t, :, r] = spread(pick_u[r], u_raw[t, r])

    def spread_weight(t, r):
        w_out[t, :, r] = spread(pick_w[r], w_raw[t, r, 0:96, :])

    plane_target = lax.broadcasted_iota(jnp.int32, (plane, 8, 128), 0) * 2

    def spread_first(t, r):
        coded = jnp.broadcast_to(w_raw[0, r, 128:129, :], (8, 128)).astype(jnp.int32)
        lies, level = placed(coded // 2)
        wanted = jnp.where(
            matched & (level == zc), 2 * lies + coded % 2 - slot_of, -1000000
        )
        hot = jnp.where(wanted[None] == plane_target, 1.0, 0.0).astype(F32)
        where_to = jnp.broadcast_to(w_raw[0, r, 129:130, :], (8, 128))
        idw_out[:, r] = jnp.broadcast_to(hot_ids(hot, where_to[None]), (plane, 8, 128))
        hot = hot.reshape(plane * 8, 128).astype(BF16)
        pick_w[r, :, 0:128] = hot
        pick_w[r, :, 128:256] = hot
        w_out[0, :, r] = spread(pick_w[r], w_raw[0, r, 0:128, :])

    weights = [
        Exchange(
            w_raw, w_out, w_in, w_zss, w_zrs, w_ss, w_rs, t,
            136 if t == 0 else 96, 8 if t == 0 else 6, spread_first if t == 0 else spread_weight,
        )
        for t in range(SUBSTEPS)
    ]
    flows = [
        Exchange(u_raw, u_out, u_in, u_zss, u_zrs, u_ss, u_rs, t, 96, 6, spread_flow)
        for t in range(SUBSTEPS)
    ]

    def send_ids(g):
        plane_send(idw_out, idw_in, idw_ss, idw_rs.at[g], *GROUPS[g], 6, 2)

    def picked(id_tiles):
        first = jnp.broadcast_to(id_tiles[:, 6:7, :], id_tiles.shape)
        second = jnp.broadcast_to(id_tiles[:, 7:8, :], id_tiles.shape)
        held = jnp.where((slot_of == 0)[None], first, second)
        wanted = jnp.where(matched, index + 1, -1).astype(F32)
        return jnp.where(held == wanted[None], 1.0, 0.0).astype(F32)

    def start_flow(t, u):
        for a in range(3):
            u_raw[t, 0, a * 32 : a * 32 + 32, :] = u[a]
        flows[t].start()

    def start_weight(t, v, pushed):
        for a in range(3):
            w_raw[t, 0, a * 32 : a * 32 + 32, :] = rate * ((1.0 - rate) * v[a] + pushed[a])
        weights[t].start()

    def advance(t, v, pushed):
        block = collect(pick_ht, flows[t].receive(), True)
        updated = []
        for a in range(3):
            u = block[a * 32 : a * 32 + 32]
            updated.append(v[a] + rate * (u - v[a]) + pushed[a])
        return updated

    def halo_copy(t, first_out, tiles, first_in, px, py, pz):
        return pltpu.make_async_remote_copy(
            src_ref=halo_out.at[t, pl.ds(first_out, tiles)],
            dst_ref=halo_in.at[t, pl.ds(first_in, tiles)],
            send_sem=h_ss.at[t],
            recv_sem=h_rs.at[t],
            device_id=(px, py, pz),
            device_id_type=MESH,
        )

    def collide(t, read, flow, field):
        rho, speed = flow
        scale = 1.0 / (1.0 + 0.5 * field[3])
        force = [field[a] - field[3] * speed[a] for a in range(3)]
        target = [scale * (speed[a] + relax_time * force[a] / rho) for a in range(3)]
        square = target[0] * target[0] + target[1] * target[1] + target[2] * target[2]
        base = 1.0 - 1.5 * square
        for i in range(19):
            along = None
            for a in range(3):
                c = VELOCITIES[i][a]
                if c == 1:
                    along = target[a] if along is None else along + target[a]
                elif c == -1:
                    along = -target[a] if along is None else along - target[a]
            shape = base if along is None else base + along * (3.0 + 4.5 * along)
            f = read(i)
            post[pl.ds(i * 32, 32), :] = f - (f - WEIGHTS[i] * rho * shape) / relax_time

    def tile(i, x):
        return post[pl.ds(i * 32 + x * 8, 8), :]

    def send_halo(t):
        for n in range(5):
            halo_out[t, n] = tile(X_UP[n], 3)
            halo_out[t, 5 + n] = tile(X_DOWN[n], 0)
            half = pl.ds((n % 2) * 4, 4)
            halo_out[t, 10 + n // 2, half, :] = post[pl.ds(Y_UP[n] * 32 + 7, 4, stride=8), :]
            halo_out[t, 13 + n // 2, half, :] = post[pl.ds(Y_DOWN[n] * 32, 4, stride=8), :]
        halo_out[t, 12, 4:8, :] = jnp.zeros((4, 128), F32)
        halo_out[t, 15, 4:8, :] = jnp.zeros((4, 128), F32)
        packed = jnp.zeros((8, 128), F32)
        for n in range(5):
            for x in range(4):
                k = n * 4 + x
                up = pltpu.roll(tile(Z_UP[n], x), (k + 1) % 128, 1)
                down = pltpu.roll(tile(Z_DOWN[n], x), k, 1) if k else tile(Z_DOWN[n], x)
                packed = jnp.where(lane == k, jnp.where(gz == 0, up, down), packed)
        halo_out[t, 16] = packed
        halo_copy(t, 0, 5, 0, east, gy, gz).start()
        halo_copy(t, 5, 5, 5, west, gy, gz).start()
        halo_copy(t, 10, 3, 10, gx, north, gz).start()
        halo_copy(t, 13, 3, 13, gx, south, gz).start()
        halo_copy(t, 1, 1, 16, east, north, gz).start()
        halo_copy(t, 6, 1, 17, west, south, gz).start()
        halo_copy(t, 2, 1, 18, east, south, gz).start()
        halo_copy(t, 7, 1, 19, west, north, gz).start()
        for n, (px, py) in enumerate(across):
            halo_copy(t, 16, 1, 20 + n, px, py, beyond).start()

    def halo_whole(t):
        return pltpu.make_async_remote_copy(
            src_ref=halo_in.at[t],
            dst_ref=halo_in.at[t],
            send_sem=h_ss.at[t],
            recv_sem=h_rs.at[t],
            device_id=(gx, gy, beyond),
            device_id_type=MESH,
        )

    def stream(t, write):
        halo_whole(t).wait_recv()
        level = halo_in[t, 20]
        block_of = lane // 4
        from_west = pltpu.roll(halo_in[t, 21], 125, 1)
        from_east = pltpu.roll(halo_in[t, 22], 3, 1)
        right = jnp.where(lane % 4 == 0, from_west, pltpu.roll(level, 1, 1))
        left = jnp.where(lane % 4 == 3, from_east, pltpu.roll(level, 127, 1))
        upper = jnp.where(sub == 0, pltpu.roll(halo_in[t, 23], 1, 0), pltpu.roll(level, 1, 0))
        lower = jnp.where(sub == 7, pltpu.roll(halo_in[t, 24], 7, 0), pltpu.roll(level, 7, 0))
        ghost = jnp.where(block_of == 1, right, level)
        ghost = jnp.where(block_of == 2, left, ghost)
        ghost = jnp.where(block_of == 3, upper, ghost)
        ghost = jnp.where(block_of == 4, lower, ghost)

        for i in range(19):
            cx, cy, cz = VELOCITIES[i]
            for x in range(4):
                sx = x - cx
                inside = 0 <= sx < 4
                if inside:
                    value = tile(i, sx)
                elif cx == 1:
                    value = halo_in[t, X_UP.index(i)]
                else:
                    value = halo_in[t, 5 + X_DOWN.index(i)]
                if cy == 1:
                    n = Y_UP.index(i)
                    if inside:
                        row = jnp.broadcast_to(
                            halo_in[t, 10 + n // 2, pl.ds((n % 2) * 4 + sx, 1), :], (8, 128)
                        )
                    else:
                        row = jnp.broadcast_to(
                            halo_in[t, 16 if cx == 1 else 19, pl.ds(7, 1), :], (8, 128)
                        )
                    value = jnp.where(sub == 0, row, pltpu.roll(value, 1, 0))
                elif cy == -1:
                    n = Y_DOWN.index(i)
                    if inside:
                        row = jnp.broadcast_to(
                            halo_in[t, 13 + n // 2, pl.ds((n % 2) * 4 + sx, 1), :], (8, 128)
                        )
                    else:
                        row = jnp.broadcast_to(
                            halo_in[t, 18 if cx == 1 else 17, pl.ds(0, 1), :], (8, 128)
                        )
                    value = jnp.where(sub == 7, row, pltpu.roll(value, 7, 0))
                if cz != 0:
                    n = (Z_UP if cz == 1 else Z_DOWN).index(i)
                    k = n * 4 + x
                    edge = jnp.broadcast_to(ghost[:, k : k + 1], (8, 128))
                    wall = tile(OPPOSITE[i], x)
                    if cz == 1:
                        edge = jnp.where(gz == 1, edge, wall)
                        value = jnp.where(lane == 0, edge, pltpu.roll(value, 1, 1))
                    else:
                        edge = jnp.where(gz == 0, edge, wall)
                        value = jnp.where(lane == 127, edge, pltpu.roll(value, 127, 1))
                write(i, x, value)

    def write_next(i, x, value):
        fnow[pl.ds(i * 32 + x * 8, 8), :] = value

    def write_last(i, x, value):
        fluid[i, x] = value

    idh_whole = plane_whole(idh_out, idh_in, idh_ss, idh_rs, 0, n_z, 6, 2)
    flow_at = [flow] + [None] * SUBSTEPS
    field_at = [None] * SUBSTEPS
    velocity_at = [velocity] + [None] * SUBSTEPS
    push_at = [contact_push(velocity)] + [None] * SUBSTEPS
    solid_at = {}

    def start_weights():
        weights[0].start()
        plane_send(idh_out, idh_in, idh_ss, idh_rs, 0, n_z, 6, 2)

    def pick_for_flows():
        idh_whole.wait_recv()
        for r in range(n_z):
            hot = picked(idh_in[:, r]).reshape(plane * 8, 128).astype(BF16)
            pick_u[r, :, 0:128] = hot
            pick_u[r, :, 128:256] = hot

    def pick_for_bins():
        pick_ht[...] = flat(hot_h).T.astype(BF16)

    def pick_for_columns():
        for g in range(3):
            plane_whole(idw_out, idw_in, idw_ss, idw_rs.at[g], *GROUPS[g], 6, 2).wait_recv()
        hot_c = picked(idw_in[...].reshape(plane * n_z, 8, 128))
        pick_ct[...] = flat(hot_c).T.astype(BF16)

    def squares():
        tail = flat(w_in[0])
        tail = jnp.where(lax.broadcasted_iota(jnp.int32, tail.shape, 0) % 8 < 6, 0.0, tail)
        solid_at[2] = collect(pick_ct, tail * tail, False)[96:128]

    def fluid_first(t):
        rows = weights[t].receive()
        table = collect(pick_ct, rows, t > 0)
        if t == 0:
            solid_at[1] = table[96:128]
        parts = [table[a * 32 : a * 32 + 32] for a in range(3)]
        if t > 0:
            before = flow_at[t - 1][1]
            parts = [parts[a] + solid_at[2] * before[a] for a in range(3)]
        collide(t, read_first if t == 0 else read_next, flow_at[t], parts + [solid_at[1]])
        send_halo(t)

    def fluid_last(t):
        if t == SUBSTEPS - 1:
            stream(t, write_last)
            return
        stream(t, write_next)
        flow_at[t + 1] = moments(read_next)
        start_flow(t + 1, flow_at[t + 1][1])

    def grain(t):
        velocity_at[t + 1] = advance(t, velocity_at[t], push_at[t])
        if t < SUBSTEPS - 1:
            push_at[t + 1] = contact_push(velocity_at[t + 1])
        else:
            for a in range(3):
                grains[a] = velocity_at[t + 1][a]
        if t + 2 < SUBSTEPS:
            start_weight(t + 2, velocity_at[t + 1], push_at[t + 1])

    steps = {
        "start_w0": start_weights,
        "start_u0": lambda: start_flow(0, flow_at[0][1]),
        "start_w1": lambda: start_weight(1, velocity_at[0], push_at[0]),
        "pick_u": pick_for_flows,
        "pick_h": pick_for_bins,
        "pick_c": pick_for_columns,
        "squares": squares,
    }
    for t in range(SUBSTEPS):
        steps[f"collide{t}"] = lambda t=t: fluid_first(t)
        steps[f"stream{t}"] = lambda t=t: fluid_last(t)
        steps[f"grain{t}"] = lambda t=t: grain(t)
        for name, one in (("w", weights[t]), ("u", flows[t])):
            ids = send_ids if name == "w" and t == 0 else lambda g: None
            steps[f"own_{name}{t}"] = lambda one=one, ids=ids: (one.send(0), ids(0))
            steps[f"on_{name}{t}"] = lambda one=one: one.forward()
            steps[f"near_{name}{t}"] = lambda one=one, ids=ids: (one.near_parts(), ids(1))
            steps[f"far_{name}{t}"] = lambda one=one, ids=ids: (one.far_parts(), ids(2))

    pl.semaphore_wait(barrier, len(greeted))
    assert sorted(ORDER) == sorted(steps)
    for name in ORDER:
        steps[name]()

    idh_whole.wait_send()
    plane_whole(idw_out, idw_in, idw_ss, idw_rs.at[0], 0, n_z, 6, 2).wait_send()
    for t in range(SUBSTEPS):
        weights[t].finish()
        flows[t].finish()
        halo_whole(t).wait_send()


def solution(mesh):
    n_gx, n_gy = mesh.shape["gx"], mesh.shape["gy"]
    plane = n_gx // 8 * n_gy
    vmem = pl.BlockSpec(memory_space=pltpu.VMEM)
    smem = pl.BlockSpec(memory_space=pltpu.SMEM)
    dma = pltpu.SemaphoreType.DMA

    def body(populations, grain_velocity, grain_volume, slots, contacts, bin_cell):
        return pl.pallas_call(
            lambda *refs: kernel(n_gx, n_gy, *refs),
            out_shape=(
                jax.ShapeDtypeStruct(populations.shape, F32),
                jax.ShapeDtypeStruct(grain_velocity.shape, F32),
            ),
            in_specs=[vmem] * 5 + [smem],
            out_specs=(vmem, vmem),
            scratch_shapes=[
                pltpu.VMEM((608, 128), F32),
                pltpu.VMEM((608, 128), F32),
                pltpu.VMEM((8, plane * 8, 256), BF16),
                pltpu.VMEM((8, plane * 8, 256), BF16),
                pltpu.VMEM((128, plane * 64), BF16),
                pltpu.VMEM((128, plane * 64), BF16),
            ]
            + [pltpu.VMEM((plane, 8, 8, 128), F32)] * 4
            + [
                pltpu.VMEM((SUBSTEPS, 8, 96, 128), F32),
                pltpu.VMEM((SUBSTEPS, 8, 136, 128), F32),
            ]
            + [pltpu.VMEM((SUBSTEPS, plane, 8, 8, 128), F32)] * 4
            + [
                pltpu.VMEM((SUBSTEPS, 17, 8, 128), F32),
                pltpu.VMEM((SUBSTEPS, 25, 8, 128), F32),
                dma,
                dma,
                dma,
                dma((3,)),
            ]
            + [dma((SUBSTEPS,)), dma((SUBSTEPS, 9)), dma((SUBSTEPS,)), dma((SUBSTEPS, 3))] * 2
            + [dma((SUBSTEPS,)), dma((SUBSTEPS,))],
            compiler_params=pltpu.CompilerParams(
                collective_id=0, has_side_effects=True, vmem_limit_bytes=48 << 20
            ),
            name="bed",
        )(populations, grain_velocity, grain_volume, slots, contacts, bin_cell)

    every = ("gx", "gy", "gz")
    in_specs = (
        P(None, "gx", "gy", "gz"),
        P(None, every, None),
        P(every, None),
        P(every, None),
        P(every, None),
        P(every),
    )
    out_specs = (P(None, "gx", "gy", "gz"), P(None, every, None))
    return jax.shard_map(body, mesh=mesh, in_specs=in_specs, out_specs=out_specs, check_vma=False)
```

```python
import jax
import jax.numpy as jnp
import numpy as np
from jax import lax
from jax.experimental import pallas as pl
from jax.experimental.pallas import tpu as pltpu
from jax.sharding import PartitionSpec as P

SUBSTEPS = 4
VELOCITIES = [
    (0, 0, 0),
    (1, 0, 0), (-1, 0, 0), (0, 1, 0), (0, -1, 0), (0, 0, 1), (0, 0, -1),
    (1, 1, 0), (-1, -1, 0), (1, -1, 0), (-1, 1, 0),
    (1, 0, 1), (-1, 0, -1), (1, 0, -1), (-1, 0, 1),
    (0, 1, 1), (0, -1, -1), (0, 1, -1), (0, -1, 1),
]
WEIGHTS = [1.0 / 3.0] + [1.0 / 18.0] * 6 + [1.0 / 36.0] * 12
OPPOSITE = [0, 2, 1, 4, 3, 6, 5, 8, 7, 10, 9, 12, 11, 14, 13, 16, 15, 18, 17]
relax_time = 0.8
contact_stiffness = 0.1
drag_factor = 2.0
gravity = 0.01

X_UP = [1, 7, 9, 11, 13]
X_DOWN = [2, 8, 10, 12, 14]
Y_UP = [3, 7, 10, 15, 17]
Y_DOWN = [4, 8, 9, 16, 18]
Z_UP = [5, 11, 14, 15, 18]
Z_DOWN = [6, 13, 12, 17, 16]
SOURCE = [0, -1, 1, -2, 2, -3, 3, 4]
GROUPS = [(0, 1), (1, 4), (5, 3)]
RELAYS = [
    (0, 0, 0, 0, 1), (1, 0, 1, 0, 1), (2, 0, 2, 0, 1), (3, 0, 3, 0, 1), (4, 0, 4, 0, 1),
    (3, 1, 5, 0, 1), (4, -1, 6, 0, 1), (3, 2, 7, 0, 2), (4, -2, 7, 1, 2),
]

ORDER = [
    "start_w0", "own_w0", "relay_w0", "start_u0", "pick_u", "start_w1", "own_u0",
    "relay_u0", "own_w1", "pick_h", "relay_w1", "pick_c", "collide0", "grain0",
    "own_w2", "stream0", "own_u1", "squares", "relay_w2", "collide1", "relay_u1",
    "stream1", "own_u2", "collide2", "grain1", "own_w3", "relay_u2", "stream2",
    "relay_w3", "own_u3", "relay_u3", "collide3", "grain2", "grain3", "stream3",
]

F32 = jnp.float32
BF16 = jnp.bfloat16
MESH = pl.DeviceIdType.MESH


def split(x):
    high = x.astype(BF16)
    low = (x - high.astype(F32)).astype(BF16)
    return high, low


def kernel(
    n_gx, n_gy,
    pop, vel, vol, slots, contacts, cells,
    fluid, grains,
    post, fnow, pick_w, pick_u, pick_ht, pick_ct,
    idh_out, idh_in, idw_out, idw_in,
    u_raw, w_raw, u_out, u_in, w_out, w_in, halo_out, halo_in,
    idh_ss, idh_rs, idw_ss, idw_rs,
    u_zss, u_zrs, u_ss, u_rs, w_zss, w_zrs, w_ss, w_rs, h_ss, h_rs,
):
    n_z, n_c = 8, 2
    n_xh, n_y = n_gx // n_z, n_gy // n_c
    plane = n_xh * n_gy
    gx, gy, gz = lax.axis_index("gx"), lax.axis_index("gy"), lax.axis_index("gz")
    xh, zc, yc, cc = gx // n_z, gx % n_z, gy // n_c, gy % n_c
    me = xh * n_gy + gy

    def along_z(by):
        return (xh * n_z + (zc + by + n_z) % n_z, gy, gz)

    def in_plane(m):
        px = (xh + m // n_gy) % n_xh
        py = (yc + (m // n_c) % n_y) % n_y * n_c + (cc + m % n_c) % n_c
        return px, py

    west, east = (gx + n_gx - 1) % n_gx, (gx + 1) % n_gx
    south, north = (gy + n_gy - 1) % n_gy, (gy + 1) % n_gy
    beyond = 1 - gz
    across = [(gx, gy), (east, gy), (west, gy), (gx, north), (gx, south)]

    barrier = pltpu.get_barrier_semaphore()
    def beside(m, by):
        px, py = in_plane(m)
        return (px * n_z + (zc + by + n_z) % n_z, py, gz)

    greeted = [
        beside(m, by)
        for by in (2, -2, 1, -1, 0)
        for m in range(plane - 1, -1, -1)
        if m or by
    ]
    greeted += [(px, py, beyond) for px, py in across]
    for device in greeted:
        pl.semaphore_signal(barrier, inc=1, device_id=device, device_id_type=MESH)

    def z_copy(raw, t, source, region, by, start, rows, ss, rs, sem):
        part = pl.ds(start, rows)
        return pltpu.make_async_remote_copy(
            src_ref=raw.at[t, source, part],
            dst_ref=raw.at[t, region, part],
            send_sem=ss.at[t],
            recv_sem=rs.at[t, sem],
            device_id=along_z(by),
            device_id_type=MESH,
        )

    def plane_send(out, inn, ss, rs, first, tiles, row, rows):
        some, part = pl.ds(first, tiles), pl.ds(row, rows)
        for m in range(plane - 1, 0, -1):
            px, py = in_plane(m)
            pltpu.make_async_remote_copy(
                src_ref=out.at[some, px * n_gy + py, part],
                dst_ref=inn.at[some, me, part],
                send_sem=ss,
                recv_sem=rs,
                device_id=(px * n_z + zc, py, gz),
                device_id_type=MESH,
            ).start()
        inn[some, me] = out[some, me]

    def side_send(out, inn, ss, rs, k, row, rows):
        _, by, region, first, step = RELAYS[k]
        part = pl.ds(row, rows)
        for m in range(plane - 1, -1, -1):
            if step == 2:
                if m % 2:
                    continue
                px, py = in_plane(m)
                py = py // 2 * 2 + first
            else:
                px, py = in_plane(m)
            pltpu.make_async_remote_copy(
                src_ref=out.at[k, (px * n_gy + py) // step, part],
                dst_ref=inn.at[region, me, part],
                send_sem=ss,
                recv_sem=rs,
                device_id=(px * n_z + (zc + by + n_z) % n_z, py, gz),
                device_id_type=MESH,
            ).start()

    def plane_whole(out, inn, ss, rs, first, tiles, row, rows):
        devices = plane - 1 if first < 5 else plane
        span = (pl.ds(first, tiles), pl.ds(0, devices), pl.ds(row, rows))
        return pltpu.make_async_remote_copy(
            src_ref=out.at[span],
            dst_ref=inn.at[span],
            send_sem=ss,
            recv_sem=rs,
            device_id=(gx, gy, beyond),
            device_id_type=MESH,
        )

    sub = lax.broadcasted_iota(jnp.int32, (8, 128), 0)
    lane = lax.broadcasted_iota(jnp.int32, (8, 128), 1)
    matched = ((sub < 6) & (lane // 32 == sub % 3)) | ((sub >= 6) & (lane >= 96))
    slot_of = jnp.where(sub < 6, sub // 3, sub - 6)
    index = lane % 32

    cell = jnp.zeros((8, 128), jnp.int32)
    for b in range(32):
        cell = jnp.where(index == b, cells[b], cell)
    width = 8 * n_gy

    def source_of(c):
        column = c // 2
        return (column // width) // 4 * n_gy + (column % width) // 8

    source = source_of(cell)
    local = (cell // 2 // width) % 4 * 8 + (cell // 2 % width) % 8
    rank = jnp.zeros((8, 128), jnp.int32)
    for b in range(31):
        rank = rank + jnp.where((source == source_of(cells[b])) & (index > b), 1, 0)

    def placed(device):
        x, y = device // n_gy, device % n_gy
        return x // n_z * n_gy + y, x % n_z

    def hot_ids(hot, column):
        return jnp.sum(hot * column, axis=-1, keepdims=True)

    side, depth = placed(source)
    away = (depth - zc + n_z) % n_z
    region_of = jnp.zeros((8, 128), jnp.int32)
    for r, by in enumerate(SOURCE):
        region_of = jnp.where(away == by % n_z, r, region_of)
    code = jnp.where(matched, 2 * (region_of * plane + side) + rank - slot_of, -1000000)
    target = lax.broadcasted_iota(jnp.int32, (plane * n_z, 8, 128), 0) * 2
    hot_h = jnp.where(code[None] == target, 1.0, 0.0).astype(F32)
    column = (local + 1).astype(F32)
    idh_out[...] = jnp.broadcast_to(
        hot_ids(hot_h, column[None]), (plane * n_z, 8, 128)
    ).reshape(n_z, plane, 8, 128)

    def spread(pick, table):
        if table.shape[0] == 96:
            table = jnp.concatenate([table, jnp.zeros((32, 128), F32)], axis=0)
        high, low = split(table)
        both = jnp.concatenate([high, low], axis=0)
        rows = jnp.dot(pick, both, preferred_element_type=F32)
        return rows.reshape(-1, 8, 128)

    def collect(table, rows, masked):
        if masked:
            inside = lax.broadcasted_iota(jnp.int32, rows.shape, 0) % 8 < 6
            rows = jnp.where(inside, rows, 0.0)
        both = jnp.concatenate(split(rows), axis=1)
        sums = jnp.dot(table, both, preferred_element_type=F32)
        return sums[:, 0:128] + sums[:, 128:256]

    def columns_of(g):
        first, tiles = GROUPS[g]
        return slice(first * plane * 8, (first + tiles) * plane * 8)

    def flat(tiles):
        return tiles.reshape(plane * n_z * 8, 128)

    live = slots[...].astype(F32)
    rate = drag_factor * vol[...] * live
    links = contacts[...].astype(F32).astype(BF16)
    count = jnp.dot(links, live.astype(BF16), preferred_element_type=F32)

    def near(moving):
        high, low = split(moving)
        return jnp.dot(links, high, preferred_element_type=F32) + jnp.dot(
            links, low, preferred_element_type=F32
        )

    def contact_push(v):
        pushed = []
        for a in range(3):
            push = contact_stiffness * live * (near(v[a] * live) - count * v[a])
            pushed.append(push - gravity * live if a == 2 else push)
        return pushed

    velocity = [vel[a] for a in range(3)]
    for a in range(3):
        w_raw[0, 0, a * 32 : a * 32 + 32, :] = rate * velocity[a]
    w_raw[0, 0, 96:128, :] = rate
    w_raw[0, 0, 128:136, :] = jnp.where(sub == 0, 2 * source + rank, local + 1).astype(F32)

    def moments(read):
        rho = jnp.zeros((32, 128), F32)
        momentum = [jnp.zeros((32, 128), F32) for _ in range(3)]
        for i in range(19):
            f = read(i)
            rho = rho + f
            for a in range(3):
                if VELOCITIES[i][a] == 1:
                    momentum[a] = momentum[a] + f
                elif VELOCITIES[i][a] == -1:
                    momentum[a] = momentum[a] - f
        return rho, [m / rho for m in momentum]

    read_first = lambda i: pop[i].reshape(32, 128)
    read_next = lambda i: fnow[pl.ds(i * 32, 32), :]
    flow = moments(read_first)

    class Exchange:
        def __init__(self, raw, out, inn, zss, zrs, ss, rs, t, rows, shown, spread_one):
            self.raw, self.out, self.inn, self.t = raw, out, inn, t
            self.z_sems, self.p_sems = (zss, zrs), (ss, rs)
            self.rows, self.shown, self.spread_one = rows, shown, spread_one

        def z(self, region, by):
            return z_copy(self.raw, self.t, 0, region, by, 0, self.rows, *self.z_sems, region)

        def start(self):
            for by, region in ((2, 3), (-2, 4), (1, 1), (-1, 2)):
                self.z(region, by).start()

        def got(self, region):
            self.z(region, 1).wait_recv()

        def send(self, g):
            first, tiles = GROUPS[g]
            for k in range(first, first + tiles):
                self.spread_one(self.t, k)
            plane_send(
                self.out.at[self.t], self.inn.at[self.t], self.p_sems[0].at[self.t, 0],
                self.p_sems[1].at[self.t, g], first, tiles, 0, self.shown,
            )

        def send_far(self, k):
            self.spread_one(self.t, k)
            side_send(
                self.out.at[self.t], self.inn.at[self.t], self.p_sems[0].at[self.t, 1],
                self.p_sems[1].at[self.t, 2], k, 0, self.shown,
            )

        def relay(self):
            self.got(3)
            self.send_far(7)
            self.send_far(5)
            self.got(4)
            self.send_far(8)
            self.send_far(6)
            self.got(1)
            self.got(2)
            self.send(1)

        def whole(self, g, first, tiles):
            return plane_whole(
                self.out.at[self.t], self.inn.at[self.t], self.p_sems[0].at[self.t, g // 2],
                self.p_sems[1].at[self.t, g], first, tiles, 0, self.shown,
            )

        def collected(self, pick_t, masked):
            total = None
            for g, (first, tiles) in enumerate(GROUPS):
                self.whole(g, first, tiles).wait_recv()
                rows = self.inn[self.t, pl.ds(first, tiles)].reshape(tiles * plane * 8, 128)
                part = collect(pick_t[:, columns_of(g)], rows, masked)
                total = part if total is None else total + part
            return total

        def finish(self):
            part = (self.t, pl.ds(0, 4), pl.ds(0, self.rows))
            pltpu.make_async_remote_copy(
                src_ref=self.raw.at[part],
                dst_ref=self.raw.at[part],
                send_sem=self.z_sems[0].at[self.t],
                recv_sem=self.z_sems[1].at[self.t, 0],
                device_id=along_z(1),
                device_id_type=MESH,
            ).wait_send()
            self.whole(0, 0, 5).wait_send()
            self.whole(2, 5, 3).wait_send()

    def put(ref, index, k, value):
        if RELAYS[k][4] == 1:
            ref[index + (k,)] = value
        else:
            ref[index + (k, slice(0, plane // 2))] = value

    def pick_of(pick, k):
        return pick[k] if RELAYS[k][4] == 1 else pick[k, 0 : plane * 4]

    def keep_pick(pick, k, hot):
        rows = hot.shape[0] * 8
        hot = hot.reshape(rows, 128).astype(BF16)
        pick[k, 0:rows, 0:128] = hot
        pick[k, 0:rows, 128:256] = hot

    def spread_flow(t, k):
        put(u_out, (t,), k, spread(pick_of(pick_u, k), u_raw[t, RELAYS[k][0]]))

    def spread_weight(t, k):
        put(w_out, (t,), k, spread(pick_of(pick_w, k), w_raw[t, RELAYS[k][0], 0:96, :]))

    def spread_first(t, k):
        raw, by, _, first, step = RELAYS[k]
        coded = jnp.broadcast_to(w_raw[0, raw, 128:129, :], (8, 128)).astype(jnp.int32)
        lies, level = placed(coded // 2)
        wanted = jnp.where(
            matched & (level == (zc + by + n_z) % n_z), 2 * lies + coded % 2 - slot_of, -1000000
        )
        shape = (plane // step, 8, 128)
        target = 2 * (lax.broadcasted_iota(jnp.int32, shape, 0) * step + first)
        hot = jnp.where(wanted[None] == target, 1.0, 0.0).astype(F32)
        where_to = jnp.broadcast_to(w_raw[0, raw, 129:130, :], (8, 128))
        put(idw_out, (), k, jnp.broadcast_to(hot_ids(hot, where_to[None]), shape))
        keep_pick(pick_w, k, hot)
        put(w_out, (0,), k, spread(pick_of(pick_w, k), w_raw[0, raw, 0:128, :]))

    weights = [
        Exchange(
            w_raw, w_out, w_in, w_zss, w_zrs, w_ss, w_rs, t,
            136 if t == 0 else 96, 8 if t == 0 else 6, spread_first if t == 0 else spread_weight,
        )
        for t in range(SUBSTEPS)
    ]
    flows = [
        Exchange(u_raw, u_out, u_in, u_zss, u_zrs, u_ss, u_rs, t, 96, 6, spread_flow)
        for t in range(SUBSTEPS)
    ]

    def send_ids(g):
        plane_send(idw_out, idw_in, idw_ss.at[0], idw_rs.at[g], *GROUPS[g], 6, 2)

    def send_ids_far():
        for k in range(5, 9):
            side_send(idw_out, idw_in, idw_ss.at[1], idw_rs.at[2], k, 6, 2)

    def picked(id_tiles):
        first = jnp.broadcast_to(id_tiles[:, 6:7, :], id_tiles.shape)
        second = jnp.broadcast_to(id_tiles[:, 7:8, :], id_tiles.shape)
        held = jnp.where((slot_of == 0)[None], first, second)
        wanted = jnp.where(matched, index + 1, -1).astype(F32)
        return jnp.where(held == wanted[None], 1.0, 0.0).astype(F32)

    def start_flow(t, u):
        for a in range(3):
            u_raw[t, 0, a * 32 : a * 32 + 32, :] = u[a]
        flows[t].start()

    def start_weight(t, v, pushed):
        for a in range(3):
            w_raw[t, 0, a * 32 : a * 32 + 32, :] = rate * ((1.0 - rate) * v[a] + pushed[a])
        weights[t].start()

    def advance(t, v, pushed):
        block = flows[t].collected(pick_ht, True)
        updated = []
        for a in range(3):
            u = block[a * 32 : a * 32 + 32]
            updated.append(v[a] + rate * (u - v[a]) + pushed[a])
        return updated

    def halo_copy(t, first_out, tiles, first_in, px, py, pz):
        return pltpu.make_async_remote_copy(
            src_ref=halo_out.at[t, pl.ds(first_out, tiles)],
            dst_ref=halo_in.at[t, pl.ds(first_in, tiles)],
            send_sem=h_ss.at[t],
            recv_sem=h_rs.at[t],
            device_id=(px, py, pz),
            device_id_type=MESH,
        )

    def collide(t, read, flow, field):
        rho, speed = flow
        scale = 1.0 / (1.0 + 0.5 * field[3])
        force = [field[a] - field[3] * speed[a] for a in range(3)]
        target = [scale * (speed[a] + relax_time * force[a] / rho) for a in range(3)]
        square = target[0] * target[0] + target[1] * target[1] + target[2] * target[2]
        base = 1.0 - 1.5 * square
        for i in range(19):
            along = None
            for a in range(3):
                c = VELOCITIES[i][a]
                if c == 1:
                    along = target[a] if along is None else along + target[a]
                elif c == -1:
                    along = -target[a] if along is None else along - target[a]
            shape = base if along is None else base + along * (3.0 + 4.5 * along)
            f = read(i)
            post[pl.ds(i * 32, 32), :] = f - (f - WEIGHTS[i] * rho * shape) / relax_time

    def tile(i, x):
        return post[pl.ds(i * 32 + x * 8, 8), :]

    def send_halo(t):
        for n in range(5):
            halo_out[t, n] = tile(X_UP[n], 3)
            halo_out[t, 5 + n] = tile(X_DOWN[n], 0)
        halo_copy(t, 1, 1, 16, east, north, gz).start()
        halo_copy(t, 6, 1, 17, west, south, gz).start()
        halo_copy(t, 2, 1, 18, east, south, gz).start()
        halo_copy(t, 7, 1, 19, west, north, gz).start()
        halo_copy(t, 0, 5, 0, east, gy, gz).start()
        halo_copy(t, 5, 5, 5, west, gy, gz).start()
        for n in range(5):
            half = pl.ds((n % 2) * 4, 4)
            halo_out[t, 10 + n // 2, half, :] = post[pl.ds(Y_UP[n] * 32 + 7, 4, stride=8), :]
            halo_out[t, 13 + n // 2, half, :] = post[pl.ds(Y_DOWN[n] * 32, 4, stride=8), :]
        halo_out[t, 12, 4:8, :] = jnp.zeros((4, 128), F32)
        halo_out[t, 15, 4:8, :] = jnp.zeros((4, 128), F32)
        halo_copy(t, 10, 3, 10, gx, north, gz).start()
        halo_copy(t, 13, 3, 13, gx, south, gz).start()
        packed = jnp.zeros((8, 128), F32)
        for n in range(5):
            for x in range(4):
                k = n * 4 + x
                up = pltpu.roll(tile(Z_UP[n], x), (k + 1) % 128, 1)
                down = pltpu.roll(tile(Z_DOWN[n], x), k, 1) if k else tile(Z_DOWN[n], x)
                packed = jnp.where(lane == k, jnp.where(gz == 0, up, down), packed)
        halo_out[t, 16] = packed
        for n, (px, py) in enumerate(across):
            halo_copy(t, 16, 1, 20 + n, px, py, beyond).start()

    def halo_whole(t):
        return pltpu.make_async_remote_copy(
            src_ref=halo_in.at[t],
            dst_ref=halo_in.at[t],
            send_sem=h_ss.at[t],
            recv_sem=h_rs.at[t],
            device_id=(gx, gy, beyond),
            device_id_type=MESH,
        )

    def stream(t, write):
        halo_whole(t).wait_recv()
        level = halo_in[t, 20]
        block_of = lane // 4
        from_west = pltpu.roll(halo_in[t, 21], 125, 1)
        from_east = pltpu.roll(halo_in[t, 22], 3, 1)
        right = jnp.where(lane % 4 == 0, from_west, pltpu.roll(level, 1, 1))
        left = jnp.where(lane % 4 == 3, from_east, pltpu.roll(level, 127, 1))
        upper = jnp.where(sub == 0, pltpu.roll(halo_in[t, 23], 1, 0), pltpu.roll(level, 1, 0))
        lower = jnp.where(sub == 7, pltpu.roll(halo_in[t, 24], 7, 0), pltpu.roll(level, 7, 0))
        ghost = jnp.where(block_of == 1, right, level)
        ghost = jnp.where(block_of == 2, left, ghost)
        ghost = jnp.where(block_of == 3, upper, ghost)
        ghost = jnp.where(block_of == 4, lower, ghost)

        for i in range(19):
            cx, cy, cz = VELOCITIES[i]
            for x in range(4):
                sx = x - cx
                inside = 0 <= sx < 4
                if inside:
                    value = tile(i, sx)
                elif cx == 1:
                    value = halo_in[t, X_UP.index(i)]
                else:
                    value = halo_in[t, 5 + X_DOWN.index(i)]
                if cy == 1:
                    n = Y_UP.index(i)
                    if inside:
                        row = jnp.broadcast_to(
                            halo_in[t, 10 + n // 2, pl.ds((n % 2) * 4 + sx, 1), :], (8, 128)
                        )
                    else:
                        row = jnp.broadcast_to(
                            halo_in[t, 16 if cx == 1 else 19, pl.ds(7, 1), :], (8, 128)
                        )
                    value = jnp.where(sub == 0, row, pltpu.roll(value, 1, 0))
                elif cy == -1:
                    n = Y_DOWN.index(i)
                    if inside:
                        row = jnp.broadcast_to(
                            halo_in[t, 13 + n // 2, pl.ds((n % 2) * 4 + sx, 1), :], (8, 128)
                        )
                    else:
                        row = jnp.broadcast_to(
                            halo_in[t, 18 if cx == 1 else 17, pl.ds(0, 1), :], (8, 128)
                        )
                    value = jnp.where(sub == 7, row, pltpu.roll(value, 7, 0))
                if cz != 0:
                    n = (Z_UP if cz == 1 else Z_DOWN).index(i)
                    k = n * 4 + x
                    edge = jnp.broadcast_to(ghost[:, k : k + 1], (8, 128))
                    wall = tile(OPPOSITE[i], x)
                    if cz == 1:
                        edge = jnp.where(gz == 1, edge, wall)
                        value = jnp.where(lane == 0, edge, pltpu.roll(value, 1, 1))
                    else:
                        edge = jnp.where(gz == 0, edge, wall)
                        value = jnp.where(lane == 127, edge, pltpu.roll(value, 127, 1))
                write(i, x, value)

    def write_next(i, x, value):
        fnow[pl.ds(i * 32 + x * 8, 8), :] = value

    def write_last(i, x, value):
        fluid[i, x] = value

    idh_whole = [
        plane_whole(idh_out, idh_in, idh_ss.at[n], idh_rs.at[n], first, tiles, 6, 2)
        for n, (first, tiles) in enumerate([(0, 5), (5, 3)])
    ]
    flow_at = [flow] + [None] * SUBSTEPS
    field_at = [None] * SUBSTEPS
    velocity_at = [velocity] + [None] * SUBSTEPS
    push_at = [contact_push(velocity)] + [None] * SUBSTEPS
    solid_at = {}

    def start_weights():
        weights[0].start()
        for region, by in ((7, 4 * cc - 2), (5, -1), (6, 1)):
            for m in range(plane - 1, -1, -1):
                device = beside(m, by)
                pltpu.make_async_remote_copy(
                    src_ref=idh_out.at[region, device[0] // n_z * n_gy + device[1], pl.ds(6, 2)],
                    dst_ref=idh_in.at[region, me, pl.ds(6, 2)],
                    send_sem=idh_ss.at[1],
                    recv_sem=idh_rs.at[1],
                    device_id=device,
                    device_id_type=MESH,
                ).start()
        plane_send(idh_out, idh_in, idh_ss.at[0], idh_rs.at[0], 0, 5, 6, 2)

    def pick_for_flows():
        for whole in idh_whole:
            whole.wait_recv()
        for k, (_, _, region, first, step) in enumerate(RELAYS):
            tiles = idh_in[region]
            if step == 2:
                tiles = tiles.reshape(plane // 2, 2, 8, 128)[:, first]
            keep_pick(pick_u, k, picked(tiles))

    def pick_for_bins():
        pick_ht[...] = flat(hot_h).T.astype(BF16)

    def pick_for_columns():
        for g, (first, tiles) in enumerate(GROUPS):
            plane_whole(idw_out, idw_in, idw_ss, idw_rs.at[g], first, tiles, 6, 2).wait_recv()
            held = idw_in[pl.ds(first, tiles)].reshape(tiles * plane, 8, 128)
            hot_c = picked(held).reshape(tiles * plane * 8, 128)
            pick_ct[:, columns_of(g)] = hot_c.T.astype(BF16)

    def squares():
        tail = flat(w_in[0])
        tail = jnp.where(lax.broadcasted_iota(jnp.int32, tail.shape, 0) % 8 < 6, 0.0, tail)
        solid_at[2] = collect(pick_ct[...], tail * tail, False)[96:128]

    def fluid_first(t):
        table = weights[t].collected(pick_ct, t > 0)
        if t == 0:
            solid_at[1] = table[96:128]
        parts = [table[a * 32 : a * 32 + 32] for a in range(3)]
        if t > 0:
            before = flow_at[t - 1][1]
            parts = [parts[a] + solid_at[2] * before[a] for a in range(3)]
        collide(t, read_first if t == 0 else read_next, flow_at[t], parts + [solid_at[1]])
        send_halo(t)

    def fluid_last(t):
        if t == SUBSTEPS - 1:
            stream(t, write_last)
            return
        stream(t, write_next)
        flow_at[t + 1] = moments(read_next)
        start_flow(t + 1, flow_at[t + 1][1])

    def grain(t):
        velocity_at[t + 1] = advance(t, velocity_at[t], push_at[t])
        if t < SUBSTEPS - 1:
            push_at[t + 1] = contact_push(velocity_at[t + 1])
        else:
            for a in range(3):
                grains[a] = velocity_at[t + 1][a]
        if t + 2 < SUBSTEPS:
            start_weight(t + 2, velocity_at[t + 1], push_at[t + 1])

    steps = {
        "start_w0": start_weights,
        "start_u0": lambda: start_flow(0, flow_at[0][1]),
        "start_w1": lambda: start_weight(1, velocity_at[0], push_at[0]),
        "pick_u": pick_for_flows,
        "pick_h": pick_for_bins,
        "pick_c": pick_for_columns,
        "squares": squares,
    }
    for t in range(SUBSTEPS):
        steps[f"collide{t}"] = lambda t=t: fluid_first(t)
        steps[f"stream{t}"] = lambda t=t: fluid_last(t)
        steps[f"grain{t}"] = lambda t=t: grain(t)
        for name, one in (("w", weights[t]), ("u", flows[t])):
            first = name == "w" and t == 0
            steps[f"own_{name}{t}"] = lambda one=one, first=first: (
                one.send(0), send_ids(0) if first else None
            )
            steps[f"relay_{name}{t}"] = lambda one=one, first=first: (
                one.relay(), (send_ids_far(), send_ids(1)) if first else None
            )

    pl.semaphore_wait(barrier, len(greeted))
    assert sorted(ORDER) == sorted(steps)
    for name in ORDER:
        steps[name]()

    for whole in idh_whole:
        whole.wait_send()
    for n, (first, tiles) in enumerate([(0, 5), (5, 3)]):
        plane_whole(idw_out, idw_in, idw_ss.at[n], idw_rs.at[n], first, tiles, 6, 2).wait_send()
    for t in range(SUBSTEPS):
        weights[t].finish()
        flows[t].finish()
        halo_whole(t).wait_send()


def solution(mesh):
    n_gx, n_gy = mesh.shape["gx"], mesh.shape["gy"]
    plane = n_gx // 8 * n_gy
    vmem = pl.BlockSpec(memory_space=pltpu.VMEM)
    smem = pl.BlockSpec(memory_space=pltpu.SMEM)
    dma = pltpu.SemaphoreType.DMA

    def body(populations, grain_velocity, grain_volume, slots, contacts, bin_cell):
        return pl.pallas_call(
            lambda *refs: kernel(n_gx, n_gy, *refs),
            out_shape=(
                jax.ShapeDtypeStruct(populations.shape, F32),
                jax.ShapeDtypeStruct(grain_velocity.shape, F32),
            ),
            in_specs=[vmem] * 5 + [smem],
            out_specs=(vmem, vmem),
            scratch_shapes=[
                pltpu.VMEM((608, 128), F32),
                pltpu.VMEM((608, 128), F32),
                pltpu.VMEM((9, plane * 8, 256), BF16),
                pltpu.VMEM((9, plane * 8, 256), BF16),
                pltpu.VMEM((128, plane * 64), BF16),
                pltpu.VMEM((128, plane * 64), BF16),
            ]
            + [pltpu.VMEM((n, plane, 8, 128), F32) for n in (8, 8, 9, 8)]
            + [
                pltpu.VMEM((SUBSTEPS, 5, 96, 128), F32),
                pltpu.VMEM((SUBSTEPS, 5, 136, 128), F32),
            ]
            + [pltpu.VMEM((SUBSTEPS, n, plane, 8, 128), F32) for n in (9, 8, 9, 8)]
            + [
                pltpu.VMEM((SUBSTEPS, 17, 8, 128), F32),
                pltpu.VMEM((SUBSTEPS, 25, 8, 128), F32),
                dma((2,)),
                dma((2,)),
                dma((2,)),
                dma((3,)),
            ]
            + [dma((SUBSTEPS,)), dma((SUBSTEPS, 5)), dma((SUBSTEPS, 2)), dma((SUBSTEPS, 3))] * 2
            + [dma((SUBSTEPS,)), dma((SUBSTEPS,))],
            compiler_params=pltpu.CompilerParams(
                collective_id=0, has_side_effects=True, vmem_limit_bytes=48 << 20
            ),
            name="bed",
        )(populations, grain_velocity, grain_volume, slots, contacts, bin_cell)

    every = ("gx", "gy", "gz")
    in_specs = (
        P(None, "gx", "gy", "gz"),
        P(None, every, None),
        P(every, None),
        P(every, None),
        P(every, None),
        P(every),
    )
    out_specs = (P(None, "gx", "gy", "gz"), P(None, every, None))
    return jax.shard_map(body, mesh=mesh, in_specs=in_specs, out_specs=out_specs, check_vma=False)
```

```python
import jax
import jax.numpy as jnp
import numpy as np
from jax import lax
from jax.experimental import pallas as pl
from jax.experimental.pallas import tpu as pltpu
from jax.sharding import PartitionSpec as P

SUBSTEPS = 4
VELOCITIES = [
    (0, 0, 0),
    (1, 0, 0), (-1, 0, 0), (0, 1, 0), (0, -1, 0), (0, 0, 1), (0, 0, -1),
    (1, 1, 0), (-1, -1, 0), (1, -1, 0), (-1, 1, 0),
    (1, 0, 1), (-1, 0, -1), (1, 0, -1), (-1, 0, 1),
    (0, 1, 1), (0, -1, -1), (0, 1, -1), (0, -1, 1),
]
WEIGHTS = [1.0 / 3.0] + [1.0 / 18.0] * 6 + [1.0 / 36.0] * 12
OPPOSITE = [0, 2, 1, 4, 3, 6, 5, 8, 7, 10, 9, 12, 11, 14, 13, 16, 15, 18, 17]
relax_time = 0.8
contact_stiffness = 0.1
drag_factor = 2.0
gravity = 0.01

X_UP = [1, 7, 9, 11, 13]
X_DOWN = [2, 8, 10, 12, 14]
Y_UP = [3, 7, 10, 15, 17]
Y_DOWN = [4, 8, 9, 16, 18]
Z_UP = [5, 11, 14, 15, 18]
Z_DOWN = [6, 13, 12, 17, 16]
SOURCE = [0, -1, 1, -2, 2, -3, 3, 4]
GROUPS = [(0, 1), (1, 4), (5, 3)]
RELAYS = [
    (0, 0, 0, 0, 1), (1, 0, 1, 0, 1), (2, 0, 2, 0, 1), (3, 0, 3, 0, 1), (4, 0, 4, 0, 1),
    (3, 1, 5, 0, 1), (4, -1, 6, 0, 1), (3, 2, 7, 0, 2), (4, -2, 7, 1, 2),
]

ORDER = [
    "start_w0", "start_u0", "own_w0", "relay_w0", "start_w1", "pick_u", "own_u0",
    "relay_u0", "own_w1", "pick_h", "pick_c", "relay_w1", "collide0", "grain0",
    "own_w2", "stream0", "own_u1", "squares", "relay_w2", "collide1", "relay_u1",
    "stream1", "own_u2", "collide2", "grain1", "own_w3", "relay_u2", "stream2",
    "relay_w3", "own_u3", "relay_u3", "collide3", "grain2", "grain3", "stream3",
]

F32 = jnp.float32
BF16 = jnp.bfloat16
MESH = pl.DeviceIdType.MESH


def split(x):
    high = x.astype(BF16)
    low = (x - high.astype(F32)).astype(BF16)
    return high, low


def kernel(
    n_gx, n_gy,
    pop, vel, vol, slots, contacts, cells,
    fluid, grains,
    post, fnow, pick_w, pick_u, pick_ht, pick_ct,
    idh_out, idh_in, idw_out, idw_in,
    u_raw, w_raw, u_out, u_in, w_out, w_in, halo_out, halo_in,
    idh_ss, idh_rs, idw_ss, idw_rs,
    u_zss, u_zrs, u_ss, u_rs, w_zss, w_zrs, w_ss, w_rs, h_ss, h_rs,
):
    n_z, n_c = 8, 2
    n_xh, n_y = n_gx // n_z, n_gy // n_c
    plane = n_xh * n_gy
    gx, gy, gz = lax.axis_index("gx"), lax.axis_index("gy"), lax.axis_index("gz")
    xh, zc, yc, cc = gx // n_z, gx % n_z, gy // n_c, gy % n_c
    me = xh * n_gy + gy

    def along_z(by):
        return (xh * n_z + (zc + by + n_z) % n_z, gy, gz)

    def in_plane(m):
        px = (xh + m // n_gy) % n_xh
        py = (yc + (m // n_c) % n_y) % n_y * n_c + (cc + m % n_c) % n_c
        return px, py

    west, east = (gx + n_gx - 1) % n_gx, (gx + 1) % n_gx
    south, north = (gy + n_gy - 1) % n_gy, (gy + 1) % n_gy
    beyond = 1 - gz
    across = [(gx, gy), (east, gy), (west, gy), (gx, north), (gx, south)]

    barrier = pltpu.get_barrier_semaphore()
    def beside(m, by):
        px, py = in_plane(m)
        return (px * n_z + (zc + by + n_z) % n_z, py, gz)

    greeted = [
        beside(m, by)
        for by in (2, -2, 1, -1, 0)
        for m in range(plane - 1, -1, -1)
        if m or by
    ]
    greeted += [(px, py, beyond) for px, py in across]
    for device in greeted:
        pl.semaphore_signal(barrier, inc=1, device_id=device, device_id_type=MESH)

    def z_copy(raw, t, source, region, by, start, rows, ss, rs, sem):
        part = pl.ds(start, rows)
        return pltpu.make_async_remote_copy(
            src_ref=raw.at[t, source, part],
            dst_ref=raw.at[t, region, part],
            send_sem=ss.at[t],
            recv_sem=rs.at[t, sem],
            device_id=along_z(by),
            device_id_type=MESH,
        )

    def plane_send(out, inn, ss, rs, first, tiles, row, rows):
        some, part = pl.ds(first, tiles), pl.ds(row, rows)
        for m in range(plane - 1, 0, -1):
            px, py = in_plane(m)
            pltpu.make_async_remote_copy(
                src_ref=out.at[some, px * n_gy + py, part],
                dst_ref=inn.at[some, me, part],
                send_sem=ss,
                recv_sem=rs,
                device_id=(px * n_z + zc, py, gz),
                device_id_type=MESH,
            ).start()
        inn[some, me] = out[some, me]

    def side_send(out, inn, ss, rs, k, row, rows):
        _, by, region, first, step = RELAYS[k]
        part = pl.ds(row, rows)
        for m in range(plane - 1, -1, -1):
            if step == 2:
                if m % 2:
                    continue
                px, py = in_plane(m)
                py = py // 2 * 2 + first
            else:
                px, py = in_plane(m)
            pltpu.make_async_remote_copy(
                src_ref=out.at[k, (px * n_gy + py) // step, part],
                dst_ref=inn.at[region, me, part],
                send_sem=ss,
                recv_sem=rs,
                device_id=(px * n_z + (zc + by + n_z) % n_z, py, gz),
                device_id_type=MESH,
            ).start()

    def plane_whole(out, inn, ss, rs, first, tiles, row, rows):
        devices = plane - 1 if first < 5 else plane
        span = (pl.ds(first, tiles), pl.ds(0, devices), pl.ds(row, rows))
        return pltpu.make_async_remote_copy(
            src_ref=out.at[span],
            dst_ref=inn.at[span],
            send_sem=ss,
            recv_sem=rs,
            device_id=(gx, gy, beyond),
            device_id_type=MESH,
        )

    sub = lax.broadcasted_iota(jnp.int32, (8, 128), 0)
    lane = lax.broadcasted_iota(jnp.int32, (8, 128), 1)
    matched = ((sub < 6) & (lane // 32 == sub % 3)) | ((sub >= 6) & (lane >= 96))
    slot_of = jnp.where(sub < 6, sub // 3, sub - 6)
    index = lane % 32

    cell = jnp.zeros((8, 128), jnp.int32)
    for b in range(32):
        cell = jnp.where(index == b, cells[b], cell)
    width = 8 * n_gy

    def source_of(c):
        column = c // 2
        return (column // width) // 4 * n_gy + (column % width) // 8

    source = source_of(cell)
    local = (cell // 2 // width) % 4 * 8 + (cell // 2 % width) % 8
    rank = jnp.zeros((8, 128), jnp.int32)
    for b in range(31):
        rank = rank + jnp.where((source == source_of(cells[b])) & (index > b), 1, 0)

    def placed(device):
        x, y = device // n_gy, device % n_gy
        return x // n_z * n_gy + y, x % n_z

    def hot_ids(hot, column):
        return jnp.sum(hot * column, axis=-1, keepdims=True)

    side, depth = placed(source)
    away = (depth - zc + n_z) % n_z
    region_of = jnp.zeros((8, 128), jnp.int32)
    for r, by in enumerate(SOURCE):
        region_of = jnp.where(away == by % n_z, r, region_of)
    code = jnp.where(matched, 2 * (region_of * plane + side) + rank - slot_of, -1000000)
    target = lax.broadcasted_iota(jnp.int32, (plane * n_z, 8, 128), 0) * 2
    hot_h = jnp.where(code[None] == target, 1.0, 0.0).astype(F32)
    column = (local + 1).astype(F32)
    idh_out[...] = jnp.broadcast_to(
        hot_ids(hot_h, column[None]), (plane * n_z, 8, 128)
    ).reshape(n_z, plane, 8, 128)

    def spread(pick, table):
        if table.shape[0] == 96:
            table = jnp.concatenate([table, jnp.zeros((32, 128), F32)], axis=0)
        high, low = split(table)
        both = jnp.concatenate([high, low], axis=0)
        rows = jnp.dot(pick, both, preferred_element_type=F32)
        return rows.reshape(-1, 8, 128)

    def collect(table, rows, masked):
        if masked:
            inside = lax.broadcasted_iota(jnp.int32, rows.shape, 0) % 8 < 6
            rows = jnp.where(inside, rows, 0.0)
        both = jnp.concatenate(split(rows), axis=1)
        sums = jnp.dot(table, both, preferred_element_type=F32)
        return sums[:, 0:128] + sums[:, 128:256]

    def columns_of(g):
        first, tiles = GROUPS[g]
        return slice(first * plane * 8, (first + tiles) * plane * 8)

    def flat(tiles):
        return tiles.reshape(plane * n_z * 8, 128)

    live = slots[...].astype(F32)
    rate = drag_factor * vol[...] * live
    links = contacts[...].astype(F32).astype(BF16)
    count = jnp.dot(links, live.astype(BF16), preferred_element_type=F32)

    def near(moving):
        high, low = split(moving)
        return jnp.dot(links, high, preferred_element_type=F32) + jnp.dot(
            links, low, preferred_element_type=F32
        )

    def contact_push(v):
        pushed = []
        for a in range(3):
            push = contact_stiffness * live * (near(v[a] * live) - count * v[a])
            pushed.append(push - gravity * live if a == 2 else push)
        return pushed

    velocity = [vel[a] for a in range(3)]
    for a in range(3):
        w_raw[0, 0, a * 32 : a * 32 + 32, :] = rate * velocity[a]
    w_raw[0, 0, 96:128, :] = rate
    w_raw[0, 0, 128:136, :] = jnp.where(sub == 0, 2 * source + rank, local + 1).astype(F32)

    def moments(read):
        rho = jnp.zeros((32, 128), F32)
        momentum = [jnp.zeros((32, 128), F32) for _ in range(3)]
        for i in range(19):
            f = read(i)
            rho = rho + f
            for a in range(3):
                if VELOCITIES[i][a] == 1:
                    momentum[a] = momentum[a] + f
                elif VELOCITIES[i][a] == -1:
                    momentum[a] = momentum[a] - f
        return rho, [m / rho for m in momentum]

    read_first = lambda i: pop[i].reshape(32, 128)
    read_next = lambda i: fnow[pl.ds(i * 32, 32), :]
    flow = moments(read_first)

    class Exchange:
        def __init__(self, raw, out, inn, zss, zrs, ss, rs, t, rows, shown, spread_one):
            self.raw, self.out, self.inn, self.t = raw, out, inn, t
            self.z_sems, self.p_sems = (zss, zrs), (ss, rs)
            self.rows, self.shown, self.spread_one = rows, shown, spread_one

        def z(self, region, by):
            return z_copy(self.raw, self.t, 0, region, by, 0, self.rows, *self.z_sems, region)

        def start(self):
            for by, region in ((2, 3), (-2, 4), (1, 1), (-1, 2)):
                self.z(region, by).start()

        def got(self, region):
            self.z(region, 1).wait_recv()

        def send(self, g):
            first, tiles = GROUPS[g]
            for k in range(first, first + tiles):
                self.spread_one(self.t, k)
            plane_send(
                self.out.at[self.t], self.inn.at[self.t], self.p_sems[0].at[self.t, 0],
                self.p_sems[1].at[self.t, g], first, tiles, 0, self.shown,
            )

        def send_far(self, k):
            self.spread_one(self.t, k)
            side_send(
                self.out.at[self.t], self.inn.at[self.t], self.p_sems[0].at[self.t, 1],
                self.p_sems[1].at[self.t, 2], k, 0, self.shown,
            )

        def relay(self):
            self.got(3)
            self.send_far(7)
            self.send_far(5)
            self.got(4)
            self.send_far(8)
            self.send_far(6)
            self.got(1)
            self.got(2)
            self.send(1)

        def whole(self, g, first, tiles):
            return plane_whole(
                self.out.at[self.t], self.inn.at[self.t], self.p_sems[0].at[self.t, g // 2],
                self.p_sems[1].at[self.t, g], first, tiles, 0, self.shown,
            )

        def collected(self, pick_t, masked):
            total = None
            for g, (first, tiles) in enumerate(GROUPS):
                self.whole(g, first, tiles).wait_recv()
                rows = self.inn[self.t, pl.ds(first, tiles)].reshape(tiles * plane * 8, 128)
                part = collect(pick_t[:, columns_of(g)], rows, masked)
                total = part if total is None else total + part
            return total

        def finish(self):
            part = (self.t, pl.ds(0, 4), pl.ds(0, self.rows))
            pltpu.make_async_remote_copy(
                src_ref=self.raw.at[part],
                dst_ref=self.raw.at[part],
                send_sem=self.z_sems[0].at[self.t],
                recv_sem=self.z_sems[1].at[self.t, 0],
                device_id=along_z(1),
                device_id_type=MESH,
            ).wait_send()
            self.whole(0, 0, 5).wait_send()
            self.whole(2, 5, 3).wait_send()

    def put(ref, index, k, value):
        if RELAYS[k][4] == 1:
            ref[index + (k,)] = value
        else:
            ref[index + (k, slice(0, plane // 2))] = value

    def pick_of(pick, k):
        return pick[k] if RELAYS[k][4] == 1 else pick[k, 0 : plane * 4]

    def keep_pick(pick, k, hot):
        rows = hot.shape[0] * 8
        hot = hot.reshape(rows, 128).astype(BF16)
        pick[k, 0:rows, 0:128] = hot
        pick[k, 0:rows, 128:256] = hot

    def spread_flow(t, k):
        put(u_out, (t,), k, spread(pick_of(pick_u, k), u_raw[t, RELAYS[k][0]]))

    def spread_weight(t, k):
        put(w_out, (t,), k, spread(pick_of(pick_w, k), w_raw[t, RELAYS[k][0], 0:96, :]))

    def spread_first(t, k):
        raw, by, _, first, step = RELAYS[k]
        coded = jnp.broadcast_to(w_raw[0, raw, 128:129, :], (8, 128)).astype(jnp.int32)
        lies, level = placed(coded // 2)
        wanted = jnp.where(
            matched & (level == (zc + by + n_z) % n_z), 2 * lies + coded % 2 - slot_of, -1000000
        )
        shape = (plane // step, 8, 128)
        target = 2 * (lax.broadcasted_iota(jnp.int32, shape, 0) * step + first)
        hot = jnp.where(wanted[None] == target, 1.0, 0.0).astype(F32)
        where_to = jnp.broadcast_to(w_raw[0, raw, 129:130, :], (8, 128))
        put(idw_out, (), k, jnp.broadcast_to(hot_ids(hot, where_to[None]), shape))
        keep_pick(pick_w, k, hot)
        put(w_out, (0,), k, spread(pick_of(pick_w, k), w_raw[0, raw, 0:128, :]))

    weights = [
        Exchange(
            w_raw, w_out, w_in, w_zss, w_zrs, w_ss, w_rs, t,
            136 if t == 0 else 96, 8 if t == 0 else 6, spread_first if t == 0 else spread_weight,
        )
        for t in range(SUBSTEPS)
    ]
    flows = [
        Exchange(u_raw, u_out, u_in, u_zss, u_zrs, u_ss, u_rs, t, 96, 6, spread_flow)
        for t in range(SUBSTEPS)
    ]

    def send_ids(g):
        plane_send(idw_out, idw_in, idw_ss.at[0], idw_rs.at[g], *GROUPS[g], 6, 2)

    def send_ids_far():
        for k in range(5, 9):
            side_send(idw_out, idw_in, idw_ss.at[1], idw_rs.at[2], k, 6, 2)

    def picked(id_tiles):
        first = jnp.broadcast_to(id_tiles[:, 6:7, :], id_tiles.shape)
        second = jnp.broadcast_to(id_tiles[:, 7:8, :], id_tiles.shape)
        held = jnp.where((slot_of == 0)[None], first, second)
        wanted = jnp.where(matched, index + 1, -1).astype(F32)
        return jnp.where(held == wanted[None], 1.0, 0.0).astype(F32)

    def start_flow(t, u):
        for a in range(3):
            u_raw[t, 0, a * 32 : a * 32 + 32, :] = u[a]
        flows[t].start()

    def start_weight(t, v, pushed):
        for a in range(3):
            w_raw[t, 0, a * 32 : a * 32 + 32, :] = rate * ((1.0 - rate) * v[a] + pushed[a])
        weights[t].start()

    def advance(t, v, pushed):
        block = flows[t].collected(pick_ht, True)
        updated = []
        for a in range(3):
            u = block[a * 32 : a * 32 + 32]
            updated.append(v[a] + rate * (u - v[a]) + pushed[a])
        return updated

    def halo_copy(t, first_out, tiles, first_in, px, py, pz):
        return pltpu.make_async_remote_copy(
            src_ref=halo_out.at[t, pl.ds(first_out, tiles)],
            dst_ref=halo_in.at[t, pl.ds(first_in, tiles)],
            send_sem=h_ss.at[t],
            recv_sem=h_rs.at[t],
            device_id=(px, py, pz),
            device_id_type=MESH,
        )

    def collide(t, read, flow, field):
        rho, speed = flow
        scale = 1.0 / (1.0 + 0.5 * field[3])
        force = [field[a] - field[3] * speed[a] for a in range(3)]
        target = [scale * (speed[a] + relax_time * force[a] / rho) for a in range(3)]
        square = target[0] * target[0] + target[1] * target[1] + target[2] * target[2]
        base = 1.0 - 1.5 * square
        for i in range(19):
            along = None
            for a in range(3):
                c = VELOCITIES[i][a]
                if c == 1:
                    along = target[a] if along is None else along + target[a]
                elif c == -1:
                    along = -target[a] if along is None else along - target[a]
            shape = base if along is None else base + along * (3.0 + 4.5 * along)
            f = read(i)
            post[pl.ds(i * 32, 32), :] = f - (f - WEIGHTS[i] * rho * shape) / relax_time

    def tile(i, x):
        return post[pl.ds(i * 32 + x * 8, 8), :]

    def send_halo(t):
        for n in range(5):
            halo_out[t, n] = tile(X_UP[n], 3)
            halo_out[t, 5 + n] = tile(X_DOWN[n], 0)
        halo_copy(t, 1, 1, 16, east, north, gz).start()
        halo_copy(t, 6, 1, 17, west, south, gz).start()
        halo_copy(t, 2, 1, 18, east, south, gz).start()
        halo_copy(t, 7, 1, 19, west, north, gz).start()
        halo_copy(t, 0, 5, 0, east, gy, gz).start()
        halo_copy(t, 5, 5, 5, west, gy, gz).start()
        for n in range(5):
            half = pl.ds((n % 2) * 4, 4)
            halo_out[t, 10 + n // 2, half, :] = post[pl.ds(Y_UP[n] * 32 + 7, 4, stride=8), :]
            halo_out[t, 13 + n // 2, half, :] = post[pl.ds(Y_DOWN[n] * 32, 4, stride=8), :]
        halo_out[t, 12, 4:8, :] = jnp.zeros((4, 128), F32)
        halo_out[t, 15, 4:8, :] = jnp.zeros((4, 128), F32)
        halo_copy(t, 10, 3, 10, gx, north, gz).start()
        halo_copy(t, 13, 3, 13, gx, south, gz).start()
        packed = jnp.zeros((8, 128), F32)
        for n in range(5):
            for x in range(4):
                k = n * 4 + x
                up = pltpu.roll(tile(Z_UP[n], x), (k + 1) % 128, 1)
                down = pltpu.roll(tile(Z_DOWN[n], x), k, 1) if k else tile(Z_DOWN[n], x)
                packed = jnp.where(lane == k, jnp.where(gz == 0, up, down), packed)
        halo_out[t, 16] = packed
        for n, (px, py) in enumerate(across):
            halo_copy(t, 16, 1, 20 + n, px, py, beyond).start()

    def halo_whole(t):
        return pltpu.make_async_remote_copy(
            src_ref=halo_in.at[t],
            dst_ref=halo_in.at[t],
            send_sem=h_ss.at[t],
            recv_sem=h_rs.at[t],
            device_id=(gx, gy, beyond),
            device_id_type=MESH,
        )

    def stream(t, write):
        halo_whole(t).wait_recv()
        level = halo_in[t, 20]
        block_of = lane // 4
        from_west = pltpu.roll(halo_in[t, 21], 125, 1)
        from_east = pltpu.roll(halo_in[t, 22], 3, 1)
        right = jnp.where(lane % 4 == 0, from_west, pltpu.roll(level, 1, 1))
        left = jnp.where(lane % 4 == 3, from_east, pltpu.roll(level, 127, 1))
        upper = jnp.where(sub == 0, pltpu.roll(halo_in[t, 23], 1, 0), pltpu.roll(level, 1, 0))
        lower = jnp.where(sub == 7, pltpu.roll(halo_in[t, 24], 7, 0), pltpu.roll(level, 7, 0))
        ghost = jnp.where(block_of == 1, right, level)
        ghost = jnp.where(block_of == 2, left, ghost)
        ghost = jnp.where(block_of == 3, upper, ghost)
        ghost = jnp.where(block_of == 4, lower, ghost)

        for i in range(19):
            cx, cy, cz = VELOCITIES[i]
            for x in range(4):
                sx = x - cx
                inside = 0 <= sx < 4
                if inside:
                    value = tile(i, sx)
                elif cx == 1:
                    value = halo_in[t, X_UP.index(i)]
                else:
                    value = halo_in[t, 5 + X_DOWN.index(i)]
                if cy == 1:
                    n = Y_UP.index(i)
                    if inside:
                        row = jnp.broadcast_to(
                            halo_in[t, 10 + n // 2, pl.ds((n % 2) * 4 + sx, 1), :], (8, 128)
                        )
                    else:
                        row = jnp.broadcast_to(
                            halo_in[t, 16 if cx == 1 else 19, pl.ds(7, 1), :], (8, 128)
                        )
                    value = jnp.where(sub == 0, row, pltpu.roll(value, 1, 0))
                elif cy == -1:
                    n = Y_DOWN.index(i)
                    if inside:
                        row = jnp.broadcast_to(
                            halo_in[t, 13 + n // 2, pl.ds((n % 2) * 4 + sx, 1), :], (8, 128)
                        )
                    else:
                        row = jnp.broadcast_to(
                            halo_in[t, 18 if cx == 1 else 17, pl.ds(0, 1), :], (8, 128)
                        )
                    value = jnp.where(sub == 7, row, pltpu.roll(value, 7, 0))
                if cz != 0:
                    n = (Z_UP if cz == 1 else Z_DOWN).index(i)
                    k = n * 4 + x
                    edge = jnp.broadcast_to(ghost[:, k : k + 1], (8, 128))
                    wall = tile(OPPOSITE[i], x)
                    if cz == 1:
                        edge = jnp.where(gz == 1, edge, wall)
                        value = jnp.where(lane == 0, edge, pltpu.roll(value, 1, 1))
                    else:
                        edge = jnp.where(gz == 0, edge, wall)
                        value = jnp.where(lane == 127, edge, pltpu.roll(value, 127, 1))
                write(i, x, value)

    def write_next(i, x, value):
        fnow[pl.ds(i * 32 + x * 8, 8), :] = value

    def write_last(i, x, value):
        fluid[i, x] = value

    idh_whole = [
        plane_whole(idh_out, idh_in, idh_ss.at[n], idh_rs.at[n], first, tiles, 6, 2)
        for n, (first, tiles) in enumerate([(0, 5), (5, 3)])
    ]
    flow_at = [flow] + [None] * SUBSTEPS
    field_at = [None] * SUBSTEPS
    velocity_at = [velocity] + [None] * SUBSTEPS
    push_at = [contact_push(velocity)] + [None] * SUBSTEPS
    solid_at = {}

    def start_weights():
        weights[0].start()
        for region, by in ((7, 4 * cc - 2), (5, -1), (6, 1)):
            for m in range(plane - 1, -1, -1):
                device = beside(m, by)
                pltpu.make_async_remote_copy(
                    src_ref=idh_out.at[region, device[0] // n_z * n_gy + device[1], pl.ds(6, 2)],
                    dst_ref=idh_in.at[region, me, pl.ds(6, 2)],
                    send_sem=idh_ss.at[1],
                    recv_sem=idh_rs.at[1],
                    device_id=device,
                    device_id_type=MESH,
                ).start()
        plane_send(idh_out, idh_in, idh_ss.at[0], idh_rs.at[0], 0, 5, 6, 2)

    def pick_for_flows():
        for whole in idh_whole:
            whole.wait_recv()
        for k, (_, _, region, first, step) in enumerate(RELAYS):
            tiles = idh_in[region]
            if step == 2:
                tiles = tiles.reshape(plane // 2, 2, 8, 128)[:, first]
            keep_pick(pick_u, k, picked(tiles))

    def pick_for_bins():
        pick_ht[...] = flat(hot_h).T.astype(BF16)

    def pick_for_columns():
        for g, (first, tiles) in enumerate(GROUPS):
            plane_whole(idw_out, idw_in, idw_ss, idw_rs.at[g], first, tiles, 6, 2).wait_recv()
            held = idw_in[pl.ds(first, tiles)].reshape(tiles * plane, 8, 128)
            hot_c = picked(held).reshape(tiles * plane * 8, 128)
            pick_ct[:, columns_of(g)] = hot_c.T.astype(BF16)

    def squares():
        tail = flat(w_in[0])
        tail = jnp.where(lax.broadcasted_iota(jnp.int32, tail.shape, 0) % 8 < 6, 0.0, tail)
        solid_at[2] = collect(pick_ct[...], tail * tail, False)[96:128]

    def fluid_first(t):
        table = weights[t].collected(pick_ct, t > 0)
        if t == 0:
            solid_at[1] = table[96:128]
        parts = [table[a * 32 : a * 32 + 32] for a in range(3)]
        if t > 0:
            before = flow_at[t - 1][1]
            parts = [parts[a] + solid_at[2] * before[a] for a in range(3)]
        collide(t, read_first if t == 0 else read_next, flow_at[t], parts + [solid_at[1]])
        send_halo(t)

    def fluid_last(t):
        if t == SUBSTEPS - 1:
            stream(t, write_last)
            return
        stream(t, write_next)
        flow_at[t + 1] = moments(read_next)
        start_flow(t + 1, flow_at[t + 1][1])

    def grain(t):
        velocity_at[t + 1] = advance(t, velocity_at[t], push_at[t])
        if t < SUBSTEPS - 1:
            push_at[t + 1] = contact_push(velocity_at[t + 1])
        else:
            for a in range(3):
                grains[a] = velocity_at[t + 1][a]
        if t + 2 < SUBSTEPS:
            start_weight(t + 2, velocity_at[t + 1], push_at[t + 1])

    steps = {
        "start_w0": start_weights,
        "start_u0": lambda: start_flow(0, flow_at[0][1]),
        "start_w1": lambda: start_weight(1, velocity_at[0], push_at[0]),
        "pick_u": pick_for_flows,
        "pick_h": pick_for_bins,
        "pick_c": pick_for_columns,
        "squares": squares,
    }
    for t in range(SUBSTEPS):
        steps[f"collide{t}"] = lambda t=t: fluid_first(t)
        steps[f"stream{t}"] = lambda t=t: fluid_last(t)
        steps[f"grain{t}"] = lambda t=t: grain(t)
        for name, one in (("w", weights[t]), ("u", flows[t])):
            first = name == "w" and t == 0
            steps[f"own_{name}{t}"] = lambda one=one, first=first: (
                one.send(0), send_ids(0) if first else None
            )
            steps[f"relay_{name}{t}"] = lambda one=one, first=first: (
                one.relay(), (send_ids_far(), send_ids(1)) if first else None
            )

    pl.semaphore_wait(barrier, len(greeted))
    assert sorted(ORDER) == sorted(steps)
    for name in ORDER:
        steps[name]()

    for whole in idh_whole:
        whole.wait_send()
    for n, (first, tiles) in enumerate([(0, 5), (5, 3)]):
        plane_whole(idw_out, idw_in, idw_ss.at[n], idw_rs.at[n], first, tiles, 6, 2).wait_send()
    for t in range(SUBSTEPS):
        weights[t].finish()
        flows[t].finish()
        halo_whole(t).wait_send()


def solution(mesh):
    n_gx, n_gy = mesh.shape["gx"], mesh.shape["gy"]
    plane = n_gx // 8 * n_gy
    vmem = pl.BlockSpec(memory_space=pltpu.VMEM)
    smem = pl.BlockSpec(memory_space=pltpu.SMEM)
    dma = pltpu.SemaphoreType.DMA

    def body(populations, grain_velocity, grain_volume, slots, contacts, bin_cell):
        return pl.pallas_call(
            lambda *refs: kernel(n_gx, n_gy, *refs),
            out_shape=(
                jax.ShapeDtypeStruct(populations.shape, F32),
                jax.ShapeDtypeStruct(grain_velocity.shape, F32),
            ),
            in_specs=[vmem] * 5 + [smem],
            out_specs=(vmem, vmem),
            scratch_shapes=[
                pltpu.VMEM((608, 128), F32),
                pltpu.VMEM((608, 128), F32),
                pltpu.VMEM((9, plane * 8, 256), BF16),
                pltpu.VMEM((9, plane * 8, 256), BF16),
                pltpu.VMEM((128, plane * 64), BF16),
                pltpu.VMEM((128, plane * 64), BF16),
            ]
            + [pltpu.VMEM((n, plane, 8, 128), F32) for n in (8, 8, 9, 8)]
            + [
                pltpu.VMEM((SUBSTEPS, 5, 96, 128), F32),
                pltpu.VMEM((SUBSTEPS, 5, 136, 128), F32),
            ]
            + [pltpu.VMEM((SUBSTEPS, n, plane, 8, 128), F32) for n in (9, 8, 9, 8)]
            + [
                pltpu.VMEM((SUBSTEPS, 17, 8, 128), F32),
                pltpu.VMEM((SUBSTEPS, 25, 8, 128), F32),
                dma((2,)),
                dma((2,)),
                dma((2,)),
                dma((3,)),
            ]
            + [dma((SUBSTEPS,)), dma((SUBSTEPS, 5)), dma((SUBSTEPS, 2)), dma((SUBSTEPS, 3))] * 2
            + [dma((SUBSTEPS,)), dma((SUBSTEPS,))],
            compiler_params=pltpu.CompilerParams(
                collective_id=0, has_side_effects=True, vmem_limit_bytes=48 << 20
            ),
            name="bed",
        )(populations, grain_velocity, grain_volume, slots, contacts, bin_cell)

    every = ("gx", "gy", "gz")
    in_specs = (
        P(None, "gx", "gy", "gz"),
        P(None, every, None),
        P(every, None),
        P(every, None),
        P(every, None),
        P(every),
    )
    out_specs = (P(None, "gx", "gy", "gz"), P(None, every, None))
    return jax.shard_map(body, mesh=mesh, in_specs=in_specs, out_specs=out_specs, check_vma=False)
```
